512 devices in a mesh: rows: 16 (over x, y_lo, core), pairs: 32 (over y_hi, z).
Axes of the slice: x: 4, y: 8 (y_hi: 4, y_lo: 2; y = y_hi * 2 + y_lo), z: 8, core: 2. Of those that a mesh axis runs over, the one named last changes fastest.
Arguments:
- snapshots: float32 [32768, 8192], P('rows', 'pairs'), may hold values from -1600 to 1600, as said below
Outputs:
- rotated: float32 [32768, 8192], P('rows', 'pairs')
The draws below stay inside these ranges and needn't reach their ends.
Inputs may be any that keep to these rules, and one draw needn't show every extreme that they name: `snapshots`: finite real values.
All inputs are finite; a program needn't handle non-finite values.
Results may differ from the reference program's by a relative error of at most 0.00011.
Values sent between devices are 32-bit elements; how exact they have to be, the bound alone decides.
A program may use at most 64 MiB of HBM per device.

```python
import jax
import jax.numpy as jnp
from jax import lax

BLOCK = 128
STEPS = 2
NCOLS = 8192
MROWS = 32768
N_PAIRS = 32


def draw_snapshots(key, part):
    shape = (MROWS, NCOLS)
    key_base, key_row, key_col = jax.random.split(jax.random.fold_in(key, 11), 3)
    base = jnp.clip(jax.random.normal(key_base, shape, jnp.float32), -4.0, 4.0)
    top = jnp.log(10.0)
    row_scale = jnp.exp(jax.random.uniform(key_row, (MROWS, 1), jnp.float32, 0.0, 1.0) * top)
    col_scale = jnp.exp(jax.random.uniform(key_col, (1, NCOLS), jnp.float32, 0.0, 1.0) * top)
    return base * row_scale * col_scale


def setup_inputs(seed: int = 0) -> dict:
    key_of = jax.random.split(jax.random.key(seed), 2)
    snapshots = draw_snapshots(jax.random.fold_in(key_of[1], 71), 0)
    return dict(snapshots=snapshots)


def orthonormalize(pair, total):
    gram = lax.dot_general(pair, pair, (((0,), (0,)), ((), ())), precision=lax.Precision.HIGHEST) / total
    identity = jnp.eye(gram.shape[0], dtype=pair.dtype)
    level = jnp.trace(gram) / gram.shape[0]
    lower = jnp.linalg.cholesky(gram + 0.1 * level * identity)
    inverse = lax.linalg.triangular_solve(lower, identity, left_side=True, lower=True)
    return jnp.dot(pair, inverse.T, precision=lax.Precision.HIGHEST)

def reference(snapshots):
    total_rows = snapshots.shape[0]
    count = N_PAIRS
    stacked = jnp.transpose(snapshots.reshape(total_rows, count, 2 * BLOCK), (1, 0, 2))
    for step in range(STEPS):
        stacked = lax.map(lambda pair: orthonormalize(pair, total_rows), stacked)
        if step + 1 < STEPS:
            tops = stacked[:, :, :BLOCK]
            bottoms = stacked[:, :, BLOCK:]
            new_tops = jnp.concatenate([tops[0:1], bottoms[0:1], tops[1:count - 1]], axis=0)
            new_bottoms = jnp.concatenate([bottoms[1:], tops[count - 1:]], axis=0)
            stacked = jnp.concatenate([new_tops, new_bottoms], axis=2)
    return jnp.transpose(stacked, (1, 0, 2)).reshape(total_rows, count * 2 * BLOCK)
```

```python
import functools

import jax
import jax.numpy as jnp
from jax import lax
from jax.experimental import pallas as pl
from jax.experimental.pallas import tpu as pltpu
from jax.sharding import PartitionSpec as P

MESH = pl.DeviceIdType.MESH


def from_behind(value, axis, steps):
    count = lax.axis_size(axis)
    leading, last = (max(0, -steps), min(count, count - steps))
    return lax.ppermute(value, axis, [(source, source + steps) for source in range(leading, last)])


def gram_of(left, right):
    return lax.dot_general(left, right, (((0,), (0,)), ((), ())), precision=lax.Precision.HIGHEST)


def allreduce_kernel(n, chunk, g_ref, o_ref, recv, send_sem, recv_sem, send2_sem, recv2_sem):
    me = lax.axis_index("rows")
    col = lax.axis_index("pairs")

    barrier = pltpu.get_barrier_semaphore()
    for d in range(1, n):
        peer = lax.rem(me + d, n)
        pl.semaphore_signal(barrier, inc=1, device_id=(peer, col), device_id_type=MESH)
    pl.semaphore_wait(barrier, n - 1)

    scatter = []
    for d in range(1, n):
        peer = lax.rem(me + d, n)
        start = pl.multiple_of(peer * chunk, chunk)
        copy = pltpu.make_async_remote_copy(
            src_ref=g_ref.at[pl.ds(start, chunk), :],
            dst_ref=recv.at[d],
            send_sem=send_sem.at[d],
            recv_sem=recv_sem.at[d],
            device_id=(peer, col),
            device_id_type=MESH,
        )
        copy.start()
        scatter.append(copy)

    mine = pl.multiple_of(me * chunk, chunk)
    total = g_ref[pl.ds(mine, chunk), :]
    for d in range(1, n):
        scatter[d - 1].wait_recv()
        total = total + recv[d]
    o_ref[pl.ds(mine, chunk), :] = total
    for copy in scatter:
        copy.wait_send()

    gather = []
    for d in range(1, n):
        peer = lax.rem(me + d, n)
        copy = pltpu.make_async_remote_copy(
            src_ref=o_ref.at[pl.ds(mine, chunk), :],
            dst_ref=o_ref.at[pl.ds(mine, chunk), :],
            send_sem=send2_sem.at[d],
            recv_sem=recv2_sem.at[d],
            device_id=(peer, col),
            device_id_type=MESH,
        )
        copy.start()
        gather.append(copy)
    for d in range(1, n):
        source = lax.rem(me + n - d, n)
        start = pl.multiple_of(source * chunk, chunk)
        pltpu.make_async_remote_copy(
            src_ref=o_ref.at[pl.ds(start, chunk), :],
            dst_ref=o_ref.at[pl.ds(start, chunk), :],
            send_sem=send2_sem.at[d],
            recv_sem=recv2_sem.at[d],
            device_id=(source, col),
            device_id_type=MESH,
        ).wait_recv()
    for copy in gather:
        copy.wait_send()


def allreduce_rows(g):
    n = lax.axis_size("rows")
    rows, cols = g.shape
    chunk = rows // n
    return pl.pallas_call(
        functools.partial(allreduce_kernel, n, chunk),
        out_shape=jax.ShapeDtypeStruct((rows, cols), g.dtype),
        in_specs=[pl.BlockSpec(memory_space=pltpu.VMEM)],
        out_specs=pl.BlockSpec(memory_space=pltpu.VMEM),
        scratch_shapes=[
            pltpu.VMEM((n, chunk, cols), g.dtype),
            pltpu.SemaphoreType.DMA((n,)),
            pltpu.SemaphoreType.DMA((n,)),
            pltpu.SemaphoreType.DMA((n,)),
            pltpu.SemaphoreType.DMA((n,)),
        ],
        compiler_params=pltpu.CompilerParams(collective_id=0, has_side_effects=True),
    )(g)


def finish(pair, gram, total):
    scaled = gram / total
    identity = jnp.eye(gram.shape[0], dtype=pair.dtype)
    level = jnp.trace(scaled) / gram.shape[0]
    lower = jnp.linalg.cholesky(scaled + 0.1 * level * identity)
    inverse = lax.linalg.triangular_solve(lower, identity, left_side=True, lower=True)
    return jnp.dot(pair, inverse.T, precision=lax.Precision.HIGHEST)


def per_device(snapshots):
    local_rows = snapshots.shape[0]
    total = local_rows * lax.axis_size("rows")
    width = snapshots.shape[1] // 2
    count = lax.axis_size("pairs")
    index = lax.axis_index("pairs")
    first = index == 0
    last = index == count - 1
    pair = snapshots
    gram = allreduce_rows(gram_of(pair, pair))
    pair = finish(pair, gram, total)
    top = pair[:, :width]
    bottom = pair[:, width:]
    outgoing = jnp.where(first, bottom, top)
    arrived_top = from_behind(outgoing, "pairs", 1)
    arrived_bottom = from_behind(bottom, "pairs", -1)
    top_next = jnp.where(first, top, arrived_top)
    bottom_next = jnp.where(last, top, arrived_bottom)
    pair = jnp.concatenate([top_next, bottom_next], axis=1)
    gram = allreduce_rows(gram_of(pair, pair))
    pair = finish(pair, gram, total)
    return pair


def solution(mesh):
    return jax.shard_map(
        per_device,
        mesh=mesh,
        in_specs=(P("rows", "pairs"),),
        out_specs=P("rows", "pairs"),
        check_vma=False,
    )
```

```python
import functools

import jax
import jax.numpy as jnp
from jax import lax
from jax.experimental import pallas as pl
from jax.experimental.pallas import tpu as pltpu
from jax.sharding import PartitionSpec as P

MESH = pl.DeviceIdType.MESH


def from_behind(value, axis, steps):
    count = lax.axis_size(axis)
    leading, last = (max(0, -steps), min(count, count - steps))
    return lax.ppermute(value, axis, [(source, source + steps) for source in range(leading, last)])


def gram_of(left, right):
    return lax.dot_general(left, right, (((0,), (0,)), ((), ())), precision=lax.Precision.HIGHEST)


def allreduce_kernel(n, chunk, g_ref, o_ref, recv, send_sem, recv_sem, send2_sem, recv2_sem):
    me = lax.axis_index("rows")
    col = lax.axis_index("pairs")

    barrier = pltpu.get_barrier_semaphore()
    for d in range(1, n):
        peer = lax.rem(me + d, n)
        pl.semaphore_signal(barrier, inc=1, device_id=(peer, col), device_id_type=MESH)
    pl.semaphore_wait(barrier, n - 1)

    scatter = []
    for d in range(1, n):
        peer = lax.rem(me + d, n)
        start = pl.multiple_of(peer * chunk, chunk)
        copy = pltpu.make_async_remote_copy(
            src_ref=g_ref.at[pl.ds(start, chunk), :],
            dst_ref=recv.at[d],
            send_sem=send_sem.at[d],
            recv_sem=recv_sem.at[d],
            device_id=(peer, col),
            device_id_type=MESH,
        )
        copy.start()
        scatter.append(copy)

    mine = pl.multiple_of(me * chunk, chunk)
    total = g_ref[pl.ds(mine, chunk), :]
    for d in range(1, n):
        scatter[d - 1].wait_recv()
        total = total + recv[d]
    o_ref[pl.ds(mine, chunk), :] = total
    for copy in scatter:
        copy.wait_send()

    gather = []
    for d in range(1, n):
        peer = lax.rem(me + d, n)
        copy = pltpu.make_async_remote_copy(
            src_ref=o_ref.at[pl.ds(mine, chunk), :],
            dst_ref=o_ref.at[pl.ds(mine, chunk), :],
            send_sem=send2_sem.at[d],
            recv_sem=recv2_sem.at[d],
            device_id=(peer, col),
            device_id_type=MESH,
        )
        copy.start()
        gather.append(copy)
    for d in range(1, n):
        source = lax.rem(me + n - d, n)
        start = pl.multiple_of(source * chunk, chunk)
        pltpu.make_async_remote_copy(
            src_ref=o_ref.at[pl.ds(start, chunk), :],
            dst_ref=o_ref.at[pl.ds(start, chunk), :],
            send_sem=send2_sem.at[d],
            recv_sem=recv2_sem.at[d],
            device_id=(source, col),
            device_id_type=MESH,
        ).wait_recv()
    for copy in gather:
        copy.wait_send()


def allreduce_rows(g):
    n = lax.axis_size("rows")
    rows, cols = g.shape
    chunk = rows // n
    return pl.pallas_call(
        functools.partial(allreduce_kernel, n, chunk),
        out_shape=jax.ShapeDtypeStruct((rows, cols), g.dtype),
        in_specs=[pl.BlockSpec(memory_space=pltpu.VMEM)],
        out_specs=pl.BlockSpec(memory_space=pltpu.VMEM),
        scratch_shapes=[
            pltpu.VMEM((n, chunk, cols), g.dtype),
            pltpu.SemaphoreType.DMA((n,)),
            pltpu.SemaphoreType.DMA((n,)),
            pltpu.SemaphoreType.DMA((n,)),
            pltpu.SemaphoreType.DMA((n,)),
        ],
        compiler_params=pltpu.CompilerParams(collective_id=0, has_side_effects=True),
    )(g)


def whitener(scaled):
    identity = jnp.eye(scaled.shape[0], dtype=scaled.dtype)
    level = jnp.trace(scaled) / scaled.shape[0]
    lower = jnp.linalg.cholesky(scaled + 0.1 * level * identity)
    inverse = lax.linalg.triangular_solve(lower, identity, left_side=True, lower=True)
    return inverse.T


def mm(left, right):
    return jnp.dot(left, right, precision=lax.Precision.HIGHEST)


def tmm(left, right):
    return gram_of(left, right)


def per_device(snapshots):
    local_rows = snapshots.shape[0]
    total = local_rows * lax.axis_size("rows")
    width = snapshots.shape[1] // 2
    count = lax.axis_size("pairs")
    index = lax.axis_index("pairs")
    first = index == 0
    last = index == count - 1
    pair = snapshots

    raw_a = jnp.where(first, pair, from_behind(pair, "pairs", 1))
    raw_b = jnp.where(last, pair, from_behind(pair, "pairs", -1))

    gram = allreduce_rows(gram_of(pair, pair)) / total
    cross = allreduce_rows(gram_of(raw_a, raw_b)) / total

    whiten = whitener(gram)
    moment = tmm(whiten, mm(gram, whiten))
    top = jnp.concatenate([whiten[:, :width], moment[:width, :width]], axis=0)
    bottom = jnp.concatenate([whiten[:, width:], moment[width:, width:]], axis=0)
    outgoing = jnp.where(first, bottom, top)
    arrived_a = from_behind(outgoing, "pairs", 1)
    arrived_b = from_behind(bottom, "pairs", -1)
    side_a = jnp.where(first, top, arrived_a)
    side_b = jnp.where(last, top, arrived_b)
    rows = whiten.shape[0]
    x_a, m_a = side_a[:rows], side_a[rows:]
    x_b, m_b = side_b[:rows], side_b[rows:]

    off = tmm(x_a, mm(cross, x_b))
    gram2 = jnp.concatenate(
        [jnp.concatenate([m_a, off], axis=1), jnp.concatenate([off.T, m_b], axis=1)], axis=0
    )
    whiten2 = whitener(gram2)
    combined = jnp.concatenate([mm(x_a, whiten2[:width]), mm(x_b, whiten2[width:])], axis=0)
    return mm(jnp.concatenate([raw_a, raw_b], axis=1), combined)


def solution(mesh):
    return jax.shard_map(
        per_device,
        mesh=mesh,
        in_specs=(P("rows", "pairs"),),
        out_specs=P("rows", "pairs"),
        check_vma=False,
    )
```

```python
import functools

import jax
import jax.numpy as jnp
from jax import lax
from jax.experimental import pallas as pl
from jax.experimental.pallas import tpu as pltpu
from jax.sharding import PartitionSpec as P

MESH = pl.DeviceIdType.MESH


def from_behind(value, axis, steps):
    count = lax.axis_size(axis)
    leading, last = (max(0, -steps), min(count, count - steps))
    return lax.ppermute(value, axis, [(source, source + steps) for source in range(leading, last)])


def gram_of(left, right):
    return lax.dot_general(left, right, (((0,), (0,)), ((), ())), precision=lax.Precision.HIGHEST)


def allreduce_kernel(n, chunk, g_ref, o_ref, recv, send_sem, recv_sem, send2_sem, recv2_sem):
    me = lax.axis_index("rows")
    col = lax.axis_index("pairs")

    barrier = pltpu.get_barrier_semaphore()
    for d in range(1, n):
        peer = lax.rem(me + d, n)
        pl.semaphore_signal(barrier, inc=1, device_id=(peer, col), device_id_type=MESH)
    pl.semaphore_wait(barrier, n - 1)

    scatter = []
    for d in range(1, n):
        peer = lax.rem(me + d, n)
        start = pl.multiple_of(peer * chunk, chunk)
        copy = pltpu.make_async_remote_copy(
            src_ref=g_ref.at[pl.ds(start, chunk), :],
            dst_ref=recv.at[d],
            send_sem=send_sem.at[d],
            recv_sem=recv_sem.at[d],
            device_id=(peer, col),
            device_id_type=MESH,
        )
        copy.start()
        scatter.append(copy)

    mine = pl.multiple_of(me * chunk, chunk)
    total = g_ref[pl.ds(mine, chunk), :]
    for d in range(1, n):
        scatter[d - 1].wait_recv()
        total = total + recv[d]
    o_ref[pl.ds(mine, chunk), :] = total
    for copy in scatter:
        copy.wait_send()

    gather = []
    for d in range(1, n):
        peer = lax.rem(me + d, n)
        copy = pltpu.make_async_remote_copy(
            src_ref=o_ref.at[pl.ds(mine, chunk), :],
            dst_ref=o_ref.at[pl.ds(mine, chunk), :],
            send_sem=send2_sem.at[d],
            recv_sem=recv2_sem.at[d],
            device_id=(peer, col),
            device_id_type=MESH,
        )
        copy.start()
        gather.append(copy)
    for d in range(1, n):
        source = lax.rem(me + n - d, n)
        start = pl.multiple_of(source * chunk, chunk)
        pltpu.make_async_remote_copy(
            src_ref=o_ref.at[pl.ds(start, chunk), :],
            dst_ref=o_ref.at[pl.ds(start, chunk), :],
            send_sem=send2_sem.at[d],
            recv_sem=recv2_sem.at[d],
            device_id=(source, col),
            device_id_type=MESH,
        ).wait_recv()
    for copy in gather:
        copy.wait_send()


def allreduce_rows(g):
    n = lax.axis_size("rows")
    rows, cols = g.shape
    chunk = rows // n
    return pl.pallas_call(
        functools.partial(allreduce_kernel, n, chunk),
        out_shape=jax.ShapeDtypeStruct((rows, cols), g.dtype),
        in_specs=[pl.BlockSpec(memory_space=pltpu.VMEM)],
        out_specs=pl.BlockSpec(memory_space=pltpu.VMEM),
        scratch_shapes=[
            pltpu.VMEM((n, chunk, cols), g.dtype),
            pltpu.SemaphoreType.DMA((n,)),
            pltpu.SemaphoreType.DMA((n,)),
            pltpu.SemaphoreType.DMA((n,)),
            pltpu.SemaphoreType.DMA((n,)),
        ],
        compiler_params=pltpu.CompilerParams(collective_id=0, has_side_effects=True),
    )(g)


def whitener(scaled):
    identity = jnp.eye(scaled.shape[0], dtype=scaled.dtype)
    level = jnp.trace(scaled) / scaled.shape[0]
    lower = jnp.linalg.cholesky(scaled + 0.1 * level * identity)
    inverse = lax.linalg.triangular_solve(lower, identity, left_side=True, lower=True)
    return inverse.T


def mm(left, right):
    return jnp.dot(left, right, precision=lax.Precision.HIGHEST)


def tmm(left, right):
    return gram_of(left, right)


def per_device(snapshots):
    local_rows = snapshots.shape[0]
    total = local_rows * lax.axis_size("rows")
    width = snapshots.shape[1] // 2
    count = lax.axis_size("pairs")
    index = lax.axis_index("pairs")
    first = index == 0
    last = index == count - 1
    pair = snapshots

    gram = allreduce_rows(gram_of(pair, pair)) / total
    sent, gram = lax.optimization_barrier((pair, gram))
    raw_a = jnp.where(first, pair, from_behind(sent, "pairs", 1))
    raw_b = jnp.where(last, pair, from_behind(sent, "pairs", -1))

    cross = allreduce_rows(gram_of(raw_a, raw_b)) / total

    whiten = whitener(gram)
    moment = tmm(whiten, mm(gram, whiten))
    top = jnp.concatenate([whiten[:, :width], moment[:width, :width]], axis=0)
    bottom = jnp.concatenate([whiten[:, width:], moment[width:, width:]], axis=0)
    outgoing = jnp.where(first, bottom, top)
    arrived_a = from_behind(outgoing, "pairs", 1)
    arrived_b = from_behind(bottom, "pairs", -1)
    side_a = jnp.where(first, top, arrived_a)
    side_b = jnp.where(last, top, arrived_b)
    rows = whiten.shape[0]
    x_a, m_a = side_a[:rows], side_a[rows:]
    x_b, m_b = side_b[:rows], side_b[rows:]

    off = tmm(x_a, mm(cross, x_b))
    gram2 = jnp.concatenate(
        [jnp.concatenate([m_a, off], axis=1), jnp.concatenate([off.T, m_b], axis=1)], axis=0
    )
    whiten2 = whitener(gram2)
    combined = jnp.concatenate([mm(x_a, whiten2[:width]), mm(x_b, whiten2[width:])], axis=0)
    return mm(jnp.concatenate([raw_a, raw_b], axis=1), combined)


def solution(mesh):
    return jax.shard_map(
        per_device,
        mesh=mesh,
        in_specs=(P("rows", "pairs"),),
        out_specs=P("rows", "pairs"),
        check_vma=False,
    )
```

```python
import functools

import jax
import jax.numpy as jnp
from jax import lax
from jax.experimental import pallas as pl
from jax.experimental.pallas import tpu as pltpu
from jax.sharding import PartitionSpec as P

MESH = pl.DeviceIdType.MESH


def from_behind(value, axis, steps):
    count = lax.axis_size(axis)
    leading, last = (max(0, -steps), min(count, count - steps))
    return lax.ppermute(value, axis, [(source, source + steps) for source in range(leading, last)])


def gram_of(left, right):
    return lax.dot_general(left, right, (((0,), (0,)), ((), ())), precision=lax.Precision.HIGHEST)


def allreduce_kernel(n, chunk, g_ref, o_ref, recv, send_sem, recv_sem, send2_sem, recv2_sem):
    me = lax.axis_index("rows")
    col = lax.axis_index("pairs")

    barrier = pltpu.get_barrier_semaphore()
    for d in range(1, n):
        peer = lax.rem(me + d, n)
        pl.semaphore_signal(barrier, inc=1, device_id=(peer, col), device_id_type=MESH)
    pl.semaphore_wait(barrier, n - 1)

    scatter = []
    for d in range(1, n):
        peer = lax.rem(me + d, n)
        start = pl.multiple_of(peer * chunk, chunk)
        copy = pltpu.make_async_remote_copy(
            src_ref=g_ref.at[pl.ds(start, chunk), :],
            dst_ref=recv.at[d],
            send_sem=send_sem.at[d],
            recv_sem=recv_sem.at[d],
            device_id=(peer, col),
            device_id_type=MESH,
        )
        copy.start()
        scatter.append(copy)

    mine = pl.multiple_of(me * chunk, chunk)
    total = g_ref[pl.ds(mine, chunk), :]
    for d in range(1, n):
        scatter[d - 1].wait_recv()
        total = total + recv[d]
    o_ref[pl.ds(mine, chunk), :] = total
    for copy in scatter:
        copy.wait_send()

    gather = []
    for d in range(1, n):
        peer = lax.rem(me + d, n)
        copy = pltpu.make_async_remote_copy(
            src_ref=o_ref.at[pl.ds(mine, chunk), :],
            dst_ref=o_ref.at[pl.ds(mine, chunk), :],
            send_sem=send2_sem.at[d],
            recv_sem=recv2_sem.at[d],
            device_id=(peer, col),
            device_id_type=MESH,
        )
        copy.start()
        gather.append(copy)
    for d in range(1, n):
        source = lax.rem(me + n - d, n)
        start = pl.multiple_of(source * chunk, chunk)
        pltpu.make_async_remote_copy(
            src_ref=o_ref.at[pl.ds(start, chunk), :],
            dst_ref=o_ref.at[pl.ds(start, chunk), :],
            send_sem=send2_sem.at[d],
            recv_sem=recv2_sem.at[d],
            device_id=(source, col),
            device_id_type=MESH,
        ).wait_recv()
    for copy in gather:
        copy.wait_send()


def allreduce_rows(g):
    n = lax.axis_size("rows")
    rows, cols = g.shape
    chunk = rows // n
    return pl.pallas_call(
        functools.partial(allreduce_kernel, n, chunk),
        out_shape=jax.ShapeDtypeStruct((rows, cols), g.dtype),
        in_specs=[pl.BlockSpec(memory_space=pltpu.VMEM)],
        out_specs=pl.BlockSpec(memory_space=pltpu.VMEM),
        scratch_shapes=[
            pltpu.VMEM((n, chunk, cols), g.dtype),
            pltpu.SemaphoreType.DMA((n,)),
            pltpu.SemaphoreType.DMA((n,)),
            pltpu.SemaphoreType.DMA((n,)),
            pltpu.SemaphoreType.DMA((n,)),
        ],
        compiler_params=pltpu.CompilerParams(collective_id=0, has_side_effects=True),
    )(g)


def inverse_kernel(a_ref, o_ref, work):
    size = a_ref.shape[0]
    rows_i = lax.broadcasted_iota(jnp.int32, (size, size), 0)
    cols_i = lax.broadcasted_iota(jnp.int32, (size, size), 1)
    diagonal = rows_i == cols_i
    a = a_ref[...]
    level = jnp.sum(jnp.where(diagonal, a, 0.0)) / size
    work[:, :size] = a + jnp.where(diagonal, 0.1 * level, 0.0)
    work[:, size:] = jnp.where(diagonal, 1.0, 0.0).astype(work.dtype)
    tile = 8
    lanes = 128
    for block in range(size // tile):
        top = block * tile
        low = (top // lanes) * lanes
        high = size + ((top + tile + lanes - 1) // lanes) * lanes
        width = high - low
        height = size - top
        lane = lax.broadcasted_iota(jnp.int32, (1, width), 1) + low
        row_id = lax.broadcasted_iota(jnp.int32, (height, 1), 0) + top

        def step(t, carry, top=top, low=low, high=high, lane=lane, row_id=row_id):
            k = top + t
            row = work[pl.ds(k, 1), low:high]
            pivot = jnp.sum(jnp.where(lane == k, row, 0.0), axis=1, keepdims=True)
            scale = 1.0 / jnp.sqrt(pivot)
            pivot_row = row * scale
            part = work[top:, low:high]
            column = jnp.sum(jnp.where(lane == k, part, 0.0), axis=1, keepdims=True) * scale
            updated = jnp.where(row_id > k, part - column * pivot_row, part)
            work[top:, low:high] = jnp.where(row_id == k, pivot_row, updated)
            return carry

        lax.fori_loop(0, tile, step, 0)
    o_ref[...] = work[:, size:]


def lower_inverse(scaled):
    size = scaled.shape[0]
    return pl.pallas_call(
        inverse_kernel,
        out_shape=jax.ShapeDtypeStruct((size, size), scaled.dtype),
        in_specs=[pl.BlockSpec(memory_space=pltpu.VMEM)],
        out_specs=pl.BlockSpec(memory_space=pltpu.VMEM),
        scratch_shapes=[pltpu.VMEM((size, 2 * size), scaled.dtype)],
    )(scaled)


def whitener(scaled):
    return lower_inverse(scaled).T


def mm(left, right):
    return jnp.dot(left, right, precision=lax.Precision.HIGHEST)


def tmm(left, right):
    return gram_of(left, right)


def per_device(snapshots):
    local_rows = snapshots.shape[0]
    total = local_rows * lax.axis_size("rows")
    width = snapshots.shape[1] // 2
    count = lax.axis_size("pairs")
    index = lax.axis_index("pairs")
    first = index == 0
    last = index == count - 1
    pair = snapshots

    gram = allreduce_rows(gram_of(pair, pair)) / total
    sent, gram = lax.optimization_barrier((pair, gram))
    raw_a = jnp.where(first, pair, from_behind(sent, "pairs", 1))
    raw_b = jnp.where(last, pair, from_behind(sent, "pairs", -1))

    cross = allreduce_rows(gram_of(raw_a, raw_b)) / total

    whiten = whitener(gram)
    moment = tmm(whiten, mm(gram, whiten))
    top = jnp.concatenate([whiten[:, :width], moment[:width, :width]], axis=0)
    bottom = jnp.concatenate([whiten[:, width:], moment[width:, width:]], axis=0)
    outgoing = jnp.where(first, bottom, top)
    arrived_a = from_behind(outgoing, "pairs", 1)
    arrived_b = from_behind(bottom, "pairs", -1)
    side_a = jnp.where(first, top, arrived_a)
    side_b = jnp.where(last, top, arrived_b)
    rows = whiten.shape[0]
    x_a, m_a = side_a[:rows], side_a[rows:]
    x_b, m_b = side_b[:rows], side_b[rows:]

    off = tmm(x_a, mm(cross, x_b))
    gram2 = jnp.concatenate(
        [jnp.concatenate([m_a, off], axis=1), jnp.concatenate([off.T, m_b], axis=1)], axis=0
    )
    whiten2 = whitener(gram2)
    combined = jnp.concatenate([mm(x_a, whiten2[:width]), mm(x_b, whiten2[width:])], axis=0)
    return mm(jnp.concatenate([raw_a, raw_b], axis=1), combined)


def solution(mesh):
    return jax.shard_map(
        per_device,
        mesh=mesh,
        in_specs=(P("rows", "pairs"),),
        out_specs=P("rows", "pairs"),
        check_vma=False,
    )
```

```python
import functools

import jax
import jax.numpy as jnp
from jax import lax
from jax.experimental import pallas as pl
from jax.experimental.pallas import tpu as pltpu
from jax.sharding import PartitionSpec as P

MESH = pl.DeviceIdType.MESH


def from_behind(value, axis, steps):
    count = lax.axis_size(axis)
    leading, last = (max(0, -steps), min(count, count - steps))
    return lax.ppermute(value, axis, [(source, source + steps) for source in range(leading, last)])


def gram_of(left, right):
    return lax.dot_general(left, right, (((0,), (0,)), ((), ())), precision=lax.Precision.HIGHEST)


def allreduce_kernel(n, chunk, g_ref, o_ref, recv, send_sem, recv_sem, send2_sem, recv2_sem):
    me = lax.axis_index("rows")
    col = lax.axis_index("pairs")

    barrier = pltpu.get_barrier_semaphore()
    for d in range(1, n):
        peer = lax.rem(me + d, n)
        pl.semaphore_signal(barrier, inc=1, device_id=(peer, col), device_id_type=MESH)
    pl.semaphore_wait(barrier, n - 1)

    scatter = []
    for d in range(1, n):
        peer = lax.rem(me + d, n)
        start = pl.multiple_of(peer * chunk, chunk)
        copy = pltpu.make_async_remote_copy(
            src_ref=g_ref.at[pl.ds(start, chunk), :],
            dst_ref=recv.at[d],
            send_sem=send_sem.at[d],
            recv_sem=recv_sem.at[d],
            device_id=(peer, col),
            device_id_type=MESH,
        )
        copy.start()
        scatter.append(copy)

    mine = pl.multiple_of(me * chunk, chunk)
    total = g_ref[pl.ds(mine, chunk), :]
    for d in range(1, n):
        scatter[d - 1].wait_recv()
        total = total + recv[d]
    o_ref[pl.ds(mine, chunk), :] = total
    for copy in scatter:
        copy.wait_send()

    gather = []
    for d in range(1, n):
        peer = lax.rem(me + d, n)
        copy = pltpu.make_async_remote_copy(
            src_ref=o_ref.at[pl.ds(mine, chunk), :],
            dst_ref=o_ref.at[pl.ds(mine, chunk), :],
            send_sem=send2_sem.at[d],
            recv_sem=recv2_sem.at[d],
            device_id=(peer, col),
            device_id_type=MESH,
        )
        copy.start()
        gather.append(copy)
    for d in range(1, n):
        source = lax.rem(me + n - d, n)
        start = pl.multiple_of(source * chunk, chunk)
        pltpu.make_async_remote_copy(
            src_ref=o_ref.at[pl.ds(start, chunk), :],
            dst_ref=o_ref.at[pl.ds(start, chunk), :],
            send_sem=send2_sem.at[d],
            recv_sem=recv2_sem.at[d],
            device_id=(source, col),
            device_id_type=MESH,
        ).wait_recv()
    for copy in gather:
        copy.wait_send()


def allreduce_rows(g):
    n = lax.axis_size("rows")
    rows, cols = g.shape
    chunk = rows // n
    return pl.pallas_call(
        functools.partial(allreduce_kernel, n, chunk),
        out_shape=jax.ShapeDtypeStruct((rows, cols), g.dtype),
        in_specs=[pl.BlockSpec(memory_space=pltpu.VMEM)],
        out_specs=pl.BlockSpec(memory_space=pltpu.VMEM),
        scratch_shapes=[
            pltpu.VMEM((n, chunk, cols), g.dtype),
            pltpu.SemaphoreType.DMA((n,)),
            pltpu.SemaphoreType.DMA((n,)),
            pltpu.SemaphoreType.DMA((n,)),
            pltpu.SemaphoreType.DMA((n,)),
        ],
        compiler_params=pltpu.CompilerParams(collective_id=0, has_side_effects=True),
    )(g)


def inverse_kernel(a_ref, o_ref, work):
    size = a_ref.shape[0]
    rows_i = lax.broadcasted_iota(jnp.int32, (size, size), 0)
    cols_i = lax.broadcasted_iota(jnp.int32, (size, size), 1)
    diagonal = rows_i == cols_i
    a = a_ref[...]
    level = jnp.sum(jnp.where(diagonal, a, 0.0)) / size
    work[:, :size] = a + jnp.where(diagonal, 0.1 * level, 0.0)
    work[:, size:] = jnp.where(diagonal, 1.0, 0.0).astype(work.dtype)
    tile = 8
    lanes = 128
    for block in range(size // tile):
        top = block * tile
        low = (top // lanes) * lanes
        high = size + ((top + tile + lanes - 1) // lanes) * lanes
        height = size - top
        here = (top // lanes) * lanes
        lane = lax.broadcasted_iota(jnp.int32, (1, lanes), 1) + here
        row_id = lax.broadcasted_iota(jnp.int32, (height, 1), 0) + top

        def step(t, carry, top=top, low=low, high=high, here=here, lane=lane, row_id=row_id):
            k = top + t
            row = work[pl.ds(k, 1), low:high]
            pivot = jnp.sum(jnp.where(lane == k, row[:, here - low:here - low + lanes], 0.0), axis=1, keepdims=True)
            scale = 1.0 / jnp.sqrt(pivot)
            pivot_row = row * scale
            column = jnp.sum(jnp.where(lane == k, work[top:, here:here + lanes], 0.0), axis=1, keepdims=True)
            column = jnp.where(row_id > k, column * scale, 0.0)
            work[top:, low:high] = work[top:, low:high] - column * pivot_row
            work[pl.ds(k, 1), low:high] = pivot_row
            return carry

        lax.fori_loop(0, tile, step, 0)
    o_ref[...] = work[:, size:]


def lower_inverse(scaled):
    size = scaled.shape[0]
    return pl.pallas_call(
        inverse_kernel,
        out_shape=jax.ShapeDtypeStruct((size, size), scaled.dtype),
        in_specs=[pl.BlockSpec(memory_space=pltpu.VMEM)],
        out_specs=pl.BlockSpec(memory_space=pltpu.VMEM),
        scratch_shapes=[pltpu.VMEM((size, 2 * size), scaled.dtype)],
    )(scaled)


def whitener(scaled):
    return lower_inverse(scaled).T


def mm(left, right):
    return jnp.dot(left, right, precision=lax.Precision.HIGHEST)


def tmm(left, right):
    return gram_of(left, right)


def per_device(snapshots):
    local_rows = snapshots.shape[0]
    total = local_rows * lax.axis_size("rows")
    width = snapshots.shape[1] // 2
    count = lax.axis_size("pairs")
    index = lax.axis_index("pairs")
    first = index == 0
    last = index == count - 1
    pair = snapshots

    gram = allreduce_rows(gram_of(pair, pair)) / total
    sent, gram = lax.optimization_barrier((pair, gram))
    raw_a = jnp.where(first, pair, from_behind(sent, "pairs", 1))
    raw_b = jnp.where(last, pair, from_behind(sent, "pairs", -1))

    cross = allreduce_rows(gram_of(raw_a, raw_b)) / total

    whiten = whitener(gram)
    moment = tmm(whiten, mm(gram, whiten))
    top = jnp.concatenate([whiten[:, :width], moment[:width, :width]], axis=0)
    bottom = jnp.concatenate([whiten[:, width:], moment[width:, width:]], axis=0)
    outgoing = jnp.where(first, bottom, top)
    arrived_a = from_behind(outgoing, "pairs", 1)
    arrived_b = from_behind(bottom, "pairs", -1)
    side_a = jnp.where(first, top, arrived_a)
    side_b = jnp.where(last, top, arrived_b)
    rows = whiten.shape[0]
    x_a, m_a = side_a[:rows], side_a[rows:]
    x_b, m_b = side_b[:rows], side_b[rows:]

    off = tmm(x_a, mm(cross, x_b))
    gram2 = jnp.concatenate(
        [jnp.concatenate([m_a, off], axis=1), jnp.concatenate([off.T, m_b], axis=1)], axis=0
    )
    whiten2 = whitener(gram2)
    combined = jnp.concatenate([mm(x_a, whiten2[:width]), mm(x_b, whiten2[width:])], axis=0)
    return mm(jnp.concatenate([raw_a, raw_b], axis=1), combined)


def solution(mesh):
    return jax.shard_map(
        per_device,
        mesh=mesh,
        in_specs=(P("rows", "pairs"),),
        out_specs=P("rows", "pairs"),
        check_vma=False,
    )
```

```python
import functools

import jax
import jax.numpy as jnp
from jax import lax
from jax.experimental import pallas as pl
from jax.experimental.pallas import tpu as pltpu
from jax.sharding import PartitionSpec as P

MESH = pl.DeviceIdType.MESH


def from_behind(value, axis, steps):
    count = lax.axis_size(axis)
    leading, last = (max(0, -steps), min(count, count - steps))
    return lax.ppermute(value, axis, [(source, source + steps) for source in range(leading, last)])


def gram_of(left, right):
    return lax.dot_general(left, right, (((0,), (0,)), ((), ())), precision=lax.Precision.HIGHEST)


def allreduce_kernel(n, chunk, g_ref, o_ref, recv, send_sem, recv_sem, send2_sem, recv2_sem):
    me = lax.axis_index("rows")
    col = lax.axis_index("pairs")

    barrier = pltpu.get_barrier_semaphore()
    for d in range(1, n):
        peer = lax.rem(me + d, n)
        pl.semaphore_signal(barrier, inc=1, device_id=(peer, col), device_id_type=MESH)
    pl.semaphore_wait(barrier, n - 1)

    scatter = []
    for d in range(1, n):
        peer = lax.rem(me + d, n)
        start = pl.multiple_of(peer * chunk, chunk)
        copy = pltpu.make_async_remote_copy(
            src_ref=g_ref.at[pl.ds(start, chunk), :],
            dst_ref=recv.at[d],
            send_sem=send_sem.at[d],
            recv_sem=recv_sem.at[d],
            device_id=(peer, col),
            device_id_type=MESH,
        )
        copy.start()
        scatter.append(copy)

    mine = pl.multiple_of(me * chunk, chunk)
    total = g_ref[pl.ds(mine, chunk), :]
    for d in range(1, n):
        scatter[d - 1].wait_recv()
        total = total + recv[d]
    o_ref[pl.ds(mine, chunk), :] = total
    for copy in scatter:
        copy.wait_send()

    gather = []
    for d in range(1, n):
        peer = lax.rem(me + d, n)
        copy = pltpu.make_async_remote_copy(
            src_ref=o_ref.at[pl.ds(mine, chunk), :],
            dst_ref=o_ref.at[pl.ds(mine, chunk), :],
            send_sem=send2_sem.at[d],
            recv_sem=recv2_sem.at[d],
            device_id=(peer, col),
            device_id_type=MESH,
        )
        copy.start()
        gather.append(copy)
    for d in range(1, n):
        source = lax.rem(me + n - d, n)
        start = pl.multiple_of(source * chunk, chunk)
        pltpu.make_async_remote_copy(
            src_ref=o_ref.at[pl.ds(start, chunk), :],
            dst_ref=o_ref.at[pl.ds(start, chunk), :],
            send_sem=send2_sem.at[d],
            recv_sem=recv2_sem.at[d],
            device_id=(source, col),
            device_id_type=MESH,
        ).wait_recv()
    for copy in gather:
        copy.wait_send()


def allreduce_rows(g, key):
    n = lax.axis_size("rows")
    rows, cols = g.shape
    chunk = rows // n
    return pl.pallas_call(
        functools.partial(allreduce_kernel, n, chunk),
        out_shape=jax.ShapeDtypeStruct((rows, cols), g.dtype),
        in_specs=[pl.BlockSpec(memory_space=pltpu.VMEM)],
        out_specs=pl.BlockSpec(memory_space=pltpu.VMEM),
        scratch_shapes=[
            pltpu.VMEM((n, chunk, cols), g.dtype),
            pltpu.SemaphoreType.DMA((n,)),
            pltpu.SemaphoreType.DMA((n,)),
            pltpu.SemaphoreType.DMA((n,)),
            pltpu.SemaphoreType.DMA((n,)),
        ],
        compiler_params=pltpu.CompilerParams(collective_id=key, has_side_effects=True),
    )(g)


def inverse_kernel(a_ref, o_ref, work):
    size = a_ref.shape[0]
    rows_i = lax.broadcasted_iota(jnp.int32, (size, size), 0)
    cols_i = lax.broadcasted_iota(jnp.int32, (size, size), 1)
    diagonal = rows_i == cols_i
    a = a_ref[...]
    level = jnp.sum(jnp.where(diagonal, a, 0.0)) / size
    work[:, :size] = a + jnp.where(diagonal, 0.1 * level, 0.0)
    work[:, size:] = jnp.where(diagonal, 1.0, 0.0).astype(work.dtype)
    tile = 8
    lanes = 128
    for block in range(size // tile):
        top = block * tile
        low = (top // lanes) * lanes
        high = size + ((top + tile + lanes - 1) // lanes) * lanes
        height = size - top
        here = (top // lanes) * lanes
        lane = lax.broadcasted_iota(jnp.int32, (1, lanes), 1) + here
        row_id = lax.broadcasted_iota(jnp.int32, (height, 1), 0) + top

        def step(t, carry, top=top, low=low, high=high, here=here, lane=lane, row_id=row_id):
            k = top + t
            row = work[pl.ds(k, 1), low:high]
            pivot = jnp.sum(jnp.where(lane == k, row[:, here - low:here - low + lanes], 0.0), axis=1, keepdims=True)
            scale = 1.0 / jnp.sqrt(pivot)
            pivot_row = row * scale
            column = jnp.sum(jnp.where(lane == k, work[top:, here:here + lanes], 0.0), axis=1, keepdims=True)
            column = jnp.where(row_id > k, column * scale, 0.0)
            work[top:, low:high] = work[top:, low:high] - column * pivot_row
            work[pl.ds(k, 1), low:high] = pivot_row
            return carry

        lax.fori_loop(0, tile, step, 0)
    o_ref[...] = work[:, size:]


def lower_inverse(scaled):
    size = scaled.shape[0]
    return pl.pallas_call(
        inverse_kernel,
        out_shape=jax.ShapeDtypeStruct((size, size), scaled.dtype),
        in_specs=[pl.BlockSpec(memory_space=pltpu.VMEM)],
        out_specs=pl.BlockSpec(memory_space=pltpu.VMEM),
        scratch_shapes=[pltpu.VMEM((size, 2 * size), scaled.dtype)],
    )(scaled)


def whitener(scaled):
    return lower_inverse(scaled).T


def mm(left, right):
    return jnp.dot(left, right, precision=lax.Precision.HIGHEST)


def tmm(left, right):
    return gram_of(left, right)


def per_device(far, snapshots):
    local_rows = snapshots.shape[0]
    total = local_rows * lax.axis_size("rows")
    width = snapshots.shape[1] // 2
    count = lax.axis_size("pairs")
    index = lax.axis_index("pairs")
    first = index == 0
    last = index == count - 1
    pair = snapshots

    gram = allreduce_rows(gram_of(pair, pair), 0) / total
    sent, gram = lax.optimization_barrier((pair, gram))
    near_up = [(j, j + 1) for j in range(count - 1) if j not in far]
    near_down = [(j + 1, j) for j in range(count - 1) if j not in far]
    raw_a = jnp.where(first, pair, lax.ppermute(sent, "pairs", near_up))
    raw_b = jnp.where(last, pair, lax.ppermute(sent, "pairs", near_down))

    whiten = whitener(gram)
    moment = tmm(whiten, mm(gram, whiten))
    top = jnp.concatenate([whiten[:, :width], moment[:width, :width]], axis=0)
    bottom = jnp.concatenate([whiten[:, width:], moment[width:, width:]], axis=0)
    outgoing = jnp.where(first, bottom, top)
    arrived_a = from_behind(outgoing, "pairs", 1)
    arrived_b = from_behind(bottom, "pairs", -1)
    side_a = jnp.where(first, top, arrived_a)
    side_b = jnp.where(last, top, arrived_b)
    rows = whiten.shape[0]
    x_a, m_a = side_a[:rows], side_a[rows:]
    x_b, m_b = side_b[:rows], side_b[rows:]

    top_next = mm(raw_a, x_a)
    bottom_next = mm(raw_b, x_b)
    if far:
        far_a = jnp.asarray([j - 1 in far for j in range(count)])[index]
        far_b = jnp.asarray([j in far for j in range(count)])[index]
        half_a = jnp.where(first, whiten[:, width:], whiten[:, :width])
        late_a = lax.ppermute(mm(pair, half_a), "pairs", [(j, j + 1) for j in sorted(far)])
        late_b = lax.ppermute(mm(pair, whiten[:, width:]), "pairs", [(j + 1, j) for j in sorted(far)])
        top_next = jnp.where(far_a, late_a, top_next)
        bottom_next = jnp.where(far_b, late_b, bottom_next)

    off = allreduce_rows(gram_of(top_next, bottom_next), 1) / total
    gram2 = jnp.concatenate(
        [jnp.concatenate([m_a, off], axis=1), jnp.concatenate([off.T, m_b], axis=1)], axis=0
    )
    whiten2 = whitener(gram2)
    return mm(top_next, whiten2[:width]) + mm(bottom_next, whiten2[width:])


def far_links(mesh):
    far = set()
    line = mesh.devices[0]
    for j in range(len(line) - 1):
        here, there = getattr(line[j], "coords", None), getattr(line[j + 1], "coords", None)
        if here is None or there is None:
            continue
        gaps = [abs(p - q) for p, q in zip(here, there)]
        if sum(gaps) > 1:
            far.add(j)
    return frozenset(far)


def solution(mesh):
    return jax.shard_map(
        functools.partial(per_device, far_links(mesh)),
        mesh=mesh,
        in_specs=(P("rows", "pairs"),),
        out_specs=P("rows", "pairs"),
        check_vma=False,
    )
```

```python
import functools

import jax
import jax.numpy as jnp
from jax import lax
from jax.experimental import pallas as pl
from jax.experimental.pallas import tpu as pltpu
from jax.sharding import PartitionSpec as P

MESH = pl.DeviceIdType.MESH


def from_behind(value, axis, steps):
    count = lax.axis_size(axis)
    leading, last = (max(0, -steps), min(count, count - steps))
    return lax.ppermute(value, axis, [(source, source + steps) for source in range(leading, last)])


def gram_of(left, right):
    return lax.dot_general(left, right, (((0,), (0,)), ((), ())), precision=lax.Precision.HIGHEST)


def allreduce_kernel(n, chunk, g_ref, o_ref, recv, send_sem, recv_sem, send2_sem, recv2_sem):
    me = lax.axis_index("rows")
    col = lax.axis_index("pairs")

    barrier = pltpu.get_barrier_semaphore()
    for d in range(1, n):
        peer = lax.rem(me + d, n)
        pl.semaphore_signal(barrier, inc=1, device_id=(peer, col), device_id_type=MESH)
    pl.semaphore_wait(barrier, n - 1)

    scatter = []
    for d in range(1, n):
        peer = lax.rem(me + d, n)
        start = pl.multiple_of(peer * chunk, chunk)
        copy = pltpu.make_async_remote_copy(
            src_ref=g_ref.at[pl.ds(start, chunk), :],
            dst_ref=recv.at[d],
            send_sem=send_sem.at[d],
            recv_sem=recv_sem.at[d],
            device_id=(peer, col),
            device_id_type=MESH,
        )
        copy.start()
        scatter.append(copy)

    mine = pl.multiple_of(me * chunk, chunk)
    total = g_ref[pl.ds(mine, chunk), :]
    for d in range(1, n):
        scatter[d - 1].wait_recv()
        total = total + recv[d]
    o_ref[pl.ds(mine, chunk), :] = total
    for copy in scatter:
        copy.wait_send()

    gather = []
    for d in range(1, n):
        peer = lax.rem(me + d, n)
        copy = pltpu.make_async_remote_copy(
            src_ref=o_ref.at[pl.ds(mine, chunk), :],
            dst_ref=o_ref.at[pl.ds(mine, chunk), :],
            send_sem=send2_sem.at[d],
            recv_sem=recv2_sem.at[d],
            device_id=(peer, col),
            device_id_type=MESH,
        )
        copy.start()
        gather.append(copy)
    for d in range(1, n):
        source = lax.rem(me + n - d, n)
        start = pl.multiple_of(source * chunk, chunk)
        pltpu.make_async_remote_copy(
            src_ref=o_ref.at[pl.ds(start, chunk), :],
            dst_ref=o_ref.at[pl.ds(start, chunk), :],
            send_sem=send2_sem.at[d],
            recv_sem=recv2_sem.at[d],
            device_id=(source, col),
            device_id_type=MESH,
        ).wait_recv()
    for copy in gather:
        copy.wait_send()


def allreduce_rows(g):
    n = lax.axis_size("rows")
    rows, cols = g.shape
    chunk = rows // n
    return pl.pallas_call(
        functools.partial(allreduce_kernel, n, chunk),
        out_shape=jax.ShapeDtypeStruct((rows, cols), g.dtype),
        in_specs=[pl.BlockSpec(memory_space=pltpu.VMEM)],
        out_specs=pl.BlockSpec(memory_space=pltpu.VMEM),
        scratch_shapes=[
            pltpu.VMEM((n, chunk, cols), g.dtype),
            pltpu.SemaphoreType.DMA((n,)),
            pltpu.SemaphoreType.DMA((n,)),
            pltpu.SemaphoreType.DMA((n,)),
            pltpu.SemaphoreType.DMA((n,)),
        ],
        compiler_params=pltpu.CompilerParams(collective_id=0, has_side_effects=True),
    )(g)


def eliminate(work, size):
    tile = 8
    lanes = 128
    for block in range(size // tile):
        top = block * tile
        low = (top // lanes) * lanes
        high = size + min(size, ((top + tile + lanes - 1) // lanes) * lanes)
        height = size - top
        here = (top // lanes) * lanes
        lane = lax.broadcasted_iota(jnp.int32, (1, lanes), 1) + here
        row_id = lax.broadcasted_iota(jnp.int32, (height, 1), 0) + top

        def step(t, carry, top=top, low=low, high=high, here=here, lane=lane, row_id=row_id):
            k = top + t
            row = work[pl.ds(k, 1), low:high]
            pivot = jnp.sum(jnp.where(lane == k, row[:, here - low:here - low + lanes], 0.0), axis=1, keepdims=True)
            scale = 1.0 / jnp.sqrt(pivot)
            pivot_row = row * scale
            column = jnp.sum(jnp.where(lane == k, work[top:, here:here + lanes], 0.0), axis=1, keepdims=True)
            column = jnp.where(row_id > k, column * scale, 0.0)
            work[top:, low:high] = work[top:, low:high] - column * pivot_row
            work[pl.ds(k, 1), low:high] = pivot_row
            return carry

        lax.fori_loop(0, tile, step, 0)


def inverse_kernel(a_ref, o_ref, work):
    size = a_ref.shape[0]
    half = size // 2
    rows_i = lax.broadcasted_iota(jnp.int32, (size, size), 0)
    cols_i = lax.broadcasted_iota(jnp.int32, (size, size), 1)
    diagonal = rows_i == cols_i
    a = a_ref[...]
    level = jnp.sum(jnp.where(diagonal, a, 0.0)) / size
    a = a + jnp.where(diagonal, 0.1 * level, 0.0)
    eye = jnp.where(diagonal[:half, :half], 1.0, 0.0).astype(a.dtype)
    hi = lax.Precision.HIGHEST
    nt = (((1,), (1,)), ((), ()))

    work[:, :half] = a[:half, :half]
    work[:, half:] = eye
    eliminate(work, half)
    inv11 = work[:, half:]
    low21 = lax.dot_general(a[half:, :half], inv11, nt, precision=hi, preferred_element_type=jnp.float32)
    schur = a[half:, half:] - lax.dot_general(low21, low21, nt, precision=hi, preferred_element_type=jnp.float32)
    work[:, :half] = schur
    work[:, half:] = eye
    eliminate(work, half)
    inv22 = work[:, half:]
    mid = jnp.dot(inv22, low21, precision=hi, preferred_element_type=jnp.float32)
    inv21 = -jnp.dot(mid, inv11, precision=hi, preferred_element_type=jnp.float32)
    o_ref[:half, :half] = inv11
    o_ref[:half, half:] = jnp.zeros((half, half), a.dtype)
    o_ref[half:, :half] = inv21
    o_ref[half:, half:] = inv22


def lower_inverse(scaled):
    size = scaled.shape[0]
    return pl.pallas_call(
        inverse_kernel,
        out_shape=jax.ShapeDtypeStruct((size, size), scaled.dtype),
        in_specs=[pl.BlockSpec(memory_space=pltpu.VMEM)],
        out_specs=pl.BlockSpec(memory_space=pltpu.VMEM),
        scratch_shapes=[pltpu.VMEM((size // 2, size), scaled.dtype)],
    )(scaled)


def whitener(scaled):
    return lower_inverse(scaled).T


def mm(left, right):
    return jnp.dot(left, right, precision=lax.Precision.HIGHEST)


def tmm(left, right):
    return gram_of(left, right)


def per_device(snapshots):
    local_rows = snapshots.shape[0]
    total = local_rows * lax.axis_size("rows")
    width = snapshots.shape[1] // 2
    count = lax.axis_size("pairs")
    index = lax.axis_index("pairs")
    first = index == 0
    last = index == count - 1
    pair = snapshots

    gram = allreduce_rows(gram_of(pair, pair)) / total
    sent, gram = lax.optimization_barrier((pair, gram))
    raw_a = jnp.where(first, pair, from_behind(sent, "pairs", 1))
    raw_b = jnp.where(last, pair, from_behind(sent, "pairs", -1))

    cross = allreduce_rows(gram_of(raw_a, raw_b)) / total

    whiten = whitener(gram)
    moment = tmm(whiten, mm(gram, whiten))
    top = jnp.concatenate([whiten[:, :width], moment[:width, :width]], axis=0)
    bottom = jnp.concatenate([whiten[:, width:], moment[width:, width:]], axis=0)
    outgoing = jnp.where(first, bottom, top)
    arrived_a = from_behind(outgoing, "pairs", 1)
    arrived_b = from_behind(bottom, "pairs", -1)
    side_a = jnp.where(first, top, arrived_a)
    side_b = jnp.where(last, top, arrived_b)
    rows = whiten.shape[0]
    x_a, m_a = side_a[:rows], side_a[rows:]
    x_b, m_b = side_b[:rows], side_b[rows:]

    off = tmm(x_a, mm(cross, x_b))
    gram2 = jnp.concatenate(
        [jnp.concatenate([m_a, off], axis=1), jnp.concatenate([off.T, m_b], axis=1)], axis=0
    )
    whiten2 = whitener(gram2)
    combined = jnp.concatenate([mm(x_a, whiten2[:width]), mm(x_b, whiten2[width:])], axis=0)
    return mm(jnp.concatenate([raw_a, raw_b], axis=1), combined)


def solution(mesh):
    return jax.shard_map(
        per_device,
        mesh=mesh,
        in_specs=(P("rows", "pairs"),),
        out_specs=P("rows", "pairs"),
        check_vma=False,
    )
```

```python
import functools

import jax
import jax.numpy as jnp
from jax import lax
from jax.experimental import pallas as pl
from jax.experimental.pallas import tpu as pltpu
from jax.sharding import PartitionSpec as P

MESH = pl.DeviceIdType.MESH


def from_behind(value, axis, steps):
    count = lax.axis_size(axis)
    leading, last = (max(0, -steps), min(count, count - steps))
    return lax.ppermute(value, axis, [(source, source + steps) for source in range(leading, last)])


def gram_of(left, right):
    return lax.dot_general(left, right, (((0,), (0,)), ((), ())), precision=lax.Precision.HIGHEST)


def allreduce_kernel(n, chunk, g_ref, o_ref, recv, send_sem, recv_sem, send2_sem, recv2_sem):
    me = lax.axis_index("rows")
    col = lax.axis_index("pairs")

    barrier = pltpu.get_barrier_semaphore()
    for d in range(1, n):
        peer = lax.rem(me + d, n)
        pl.semaphore_signal(barrier, inc=1, device_id=(peer, col), device_id_type=MESH)
    pl.semaphore_wait(barrier, n - 1)

    scatter = []
    for d in range(1, n):
        peer = lax.rem(me + d, n)
        start = pl.multiple_of(peer * chunk, chunk)
        copy = pltpu.make_async_remote_copy(
            src_ref=g_ref.at[pl.ds(start, chunk), :],
            dst_ref=recv.at[d],
            send_sem=send_sem.at[d],
            recv_sem=recv_sem.at[d],
            device_id=(peer, col),
            device_id_type=MESH,
        )
        copy.start()
        scatter.append(copy)

    mine = pl.multiple_of(me * chunk, chunk)
    total = g_ref[pl.ds(mine, chunk), :]
    for d in range(1, n):
        scatter[d - 1].wait_recv()
        total = total + recv[d]
    o_ref[pl.ds(mine, chunk), :] = total
    for copy in scatter:
        copy.wait_send()

    gather = []
    for d in range(1, n):
        peer = lax.rem(me + d, n)
        copy = pltpu.make_async_remote_copy(
            src_ref=o_ref.at[pl.ds(mine, chunk), :],
            dst_ref=o_ref.at[pl.ds(mine, chunk), :],
            send_sem=send2_sem.at[d],
            recv_sem=recv2_sem.at[d],
            device_id=(peer, col),
            device_id_type=MESH,
        )
        copy.start()
        gather.append(copy)
    for d in range(1, n):
        source = lax.rem(me + n - d, n)
        start = pl.multiple_of(source * chunk, chunk)
        pltpu.make_async_remote_copy(
            src_ref=o_ref.at[pl.ds(start, chunk), :],
            dst_ref=o_ref.at[pl.ds(start, chunk), :],
            send_sem=send2_sem.at[d],
            recv_sem=recv2_sem.at[d],
            device_id=(source, col),
            device_id_type=MESH,
        ).wait_recv()
    for copy in gather:
        copy.wait_send()


def allreduce_rows(g, key):
    n = lax.axis_size("rows")
    rows, cols = g.shape
    chunk = rows // n
    return pl.pallas_call(
        functools.partial(allreduce_kernel, n, chunk),
        out_shape=jax.ShapeDtypeStruct((rows, cols), g.dtype),
        in_specs=[pl.BlockSpec(memory_space=pltpu.VMEM)],
        out_specs=pl.BlockSpec(memory_space=pltpu.VMEM),
        scratch_shapes=[
            pltpu.VMEM((n, chunk, cols), g.dtype),
            pltpu.SemaphoreType.DMA((n,)),
            pltpu.SemaphoreType.DMA((n,)),
            pltpu.SemaphoreType.DMA((n,)),
            pltpu.SemaphoreType.DMA((n,)),
        ],
        compiler_params=pltpu.CompilerParams(collective_id=key, has_side_effects=True),
    )(g)


def eliminate(work, size):
    tile = 8
    lanes = 128
    for block in range(size // tile):
        top = block * tile
        low = (top // lanes) * lanes
        high = size + min(size, ((top + tile + lanes - 1) // lanes) * lanes)
        height = size - top
        here = (top // lanes) * lanes
        lane = lax.broadcasted_iota(jnp.int32, (1, lanes), 1) + here
        row_id = lax.broadcasted_iota(jnp.int32, (height, 1), 0) + top

        def step(t, carry, top=top, low=low, high=high, here=here, lane=lane, row_id=row_id):
            k = top + t
            row = work[pl.ds(k, 1), low:high]
            pivot = jnp.sum(jnp.where(lane == k, row[:, here - low:here - low + lanes], 0.0), axis=1, keepdims=True)
            scale = 1.0 / jnp.sqrt(pivot)
            pivot_row = row * scale
            column = jnp.sum(jnp.where(lane == k, work[top:, here:here + lanes], 0.0), axis=1, keepdims=True)
            column = jnp.where(row_id > k, column * scale, 0.0)
            work[top:, low:high] = work[top:, low:high] - column * pivot_row
            work[pl.ds(k, 1), low:high] = pivot_row
            return carry

        lax.fori_loop(0, tile, step, 0)


def inverse_kernel(a_ref, o_ref, work):
    size = a_ref.shape[0]
    half = size // 2
    rows_i = lax.broadcasted_iota(jnp.int32, (size, size), 0)
    cols_i = lax.broadcasted_iota(jnp.int32, (size, size), 1)
    diagonal = rows_i == cols_i
    a = a_ref[...]
    level = jnp.sum(jnp.where(diagonal, a, 0.0)) / size
    a = a + jnp.where(diagonal, 0.1 * level, 0.0)
    eye = jnp.where(diagonal[:half, :half], 1.0, 0.0).astype(a.dtype)
    hi = lax.Precision.HIGHEST
    nt = (((1,), (1,)), ((), ()))

    work[:, :half] = a[:half, :half]
    work[:, half:] = eye
    eliminate(work, half)
    inv11 = work[:, half:]
    low21 = lax.dot_general(a[half:, :half], inv11, nt, precision=hi, preferred_element_type=jnp.float32)
    schur = a[half:, half:] - lax.dot_general(low21, low21, nt, precision=hi, preferred_element_type=jnp.float32)
    work[:, :half] = schur
    work[:, half:] = eye
    eliminate(work, half)
    inv22 = work[:, half:]
    mid = jnp.dot(inv22, low21, precision=hi, preferred_element_type=jnp.float32)
    inv21 = -jnp.dot(mid, inv11, precision=hi, preferred_element_type=jnp.float32)
    o_ref[:half, :half] = inv11
    o_ref[:half, half:] = jnp.zeros((half, half), a.dtype)
    o_ref[half:, :half] = inv21
    o_ref[half:, half:] = inv22


def lower_inverse(scaled):
    size = scaled.shape[0]
    return pl.pallas_call(
        inverse_kernel,
        out_shape=jax.ShapeDtypeStruct((size, size), scaled.dtype),
        in_specs=[pl.BlockSpec(memory_space=pltpu.VMEM)],
        out_specs=pl.BlockSpec(memory_space=pltpu.VMEM),
        scratch_shapes=[pltpu.VMEM((size // 2, size), scaled.dtype)],
    )(scaled)


def whitener(scaled):
    return lower_inverse(scaled).T


def mm(left, right):
    return jnp.dot(left, right, precision=lax.Precision.HIGHEST)


def tmm(left, right):
    return gram_of(left, right)


def per_device(far, snapshots):
    local_rows = snapshots.shape[0]
    total = local_rows * lax.axis_size("rows")
    width = snapshots.shape[1] // 2
    count = lax.axis_size("pairs")
    index = lax.axis_index("pairs")
    first = index == 0
    last = index == count - 1
    pair = snapshots

    gram = allreduce_rows(gram_of(pair, pair), 0) / total
    sent, gram = lax.optimization_barrier((pair, gram))
    near_up = [(j, j + 1) for j in range(count - 1) if j not in far]
    near_down = [(j + 1, j) for j in range(count - 1) if j not in far]
    raw_a = jnp.where(first, pair, lax.ppermute(sent, "pairs", near_up))
    raw_b = jnp.where(last, pair, lax.ppermute(sent, "pairs", near_down))
    head = local_rows // 2
    far_up = [(j, j + 1) for j in sorted(far)]
    far_down = [(j + 1, j) for j in sorted(far)]
    if far:
        head_a = lax.ppermute(sent[:head], "pairs", far_up)
        head_b = lax.ppermute(sent[:head], "pairs", far_down)

    whiten = whitener(gram)
    moment = tmm(whiten, mm(gram, whiten))
    top = jnp.concatenate([whiten[:, :width], moment[:width, :width]], axis=0)
    bottom = jnp.concatenate([whiten[:, width:], moment[width:, width:]], axis=0)
    outgoing = jnp.where(first, bottom, top)
    arrived_a = from_behind(outgoing, "pairs", 1)
    arrived_b = from_behind(bottom, "pairs", -1)
    side_a = jnp.where(first, top, arrived_a)
    side_b = jnp.where(last, top, arrived_b)
    rows = whiten.shape[0]
    x_a, m_a = side_a[:rows], side_a[rows:]
    x_b, m_b = side_b[:rows], side_b[rows:]

    top_next = mm(raw_a, x_a)
    bottom_next = mm(raw_b, x_b)
    if far:
        far_a = jnp.asarray([j - 1 in far for j in range(count)])[index]
        far_b = jnp.asarray([j in far for j in range(count)])[index]
        half_a = jnp.where(first, whiten[:, width:], whiten[:, :width])
        tail_a = lax.ppermute(mm(pair[head:], half_a), "pairs", far_up)
        tail_b = lax.ppermute(mm(pair[head:], whiten[:, width:]), "pairs", far_down)
        split_a = jnp.concatenate([mm(head_a, x_a), tail_a], axis=0)
        split_b = jnp.concatenate([mm(head_b, x_b), tail_b], axis=0)
        top_next = jnp.where(far_a, split_a, top_next)
        bottom_next = jnp.where(far_b, split_b, bottom_next)

    off = allreduce_rows(gram_of(top_next, bottom_next), 1) / total
    gram2 = jnp.concatenate(
        [jnp.concatenate([m_a, off], axis=1), jnp.concatenate([off.T, m_b], axis=1)], axis=0
    )
    whiten2 = whitener(gram2)
    return mm(top_next, whiten2[:width]) + mm(bottom_next, whiten2[width:])


def far_links(mesh):
    far = set()
    line = mesh.devices[0]
    for j in range(len(line) - 1):
        here, there = getattr(line[j], "coords", None), getattr(line[j + 1], "coords", None)
        if here is None or there is None:
            continue
        gaps = [abs(p - q) for p, q in zip(here, there)]
        if sum(gaps) > 1:
            far.add(j)
    return frozenset(far)


def solution(mesh):
    return jax.shard_map(
        functools.partial(per_device, far_links(mesh)),
        mesh=mesh,
        in_specs=(P("rows", "pairs"),),
        out_specs=P("rows", "pairs"),
        check_vma=False,
    )
```

```python
import functools

import jax
import jax.numpy as jnp
from jax import lax
from jax.experimental import pallas as pl
from jax.experimental.pallas import tpu as pltpu
from jax.sharding import PartitionSpec as P

MESH = pl.DeviceIdType.MESH


def from_behind(value, axis, steps):
    count = lax.axis_size(axis)
    leading, last = (max(0, -steps), min(count, count - steps))
    return lax.ppermute(value, axis, [(source, source + steps) for source in range(leading, last)])


def gram_of(left, right):
    return lax.dot_general(left, right, (((0,), (0,)), ((), ())), precision=lax.Precision.HIGHEST)


def allreduce_kernel(n, chunk, g_ref, o_ref, recv, send_sem, recv_sem, send2_sem, recv2_sem):
    me = lax.axis_index("rows")
    col = lax.axis_index("pairs")

    barrier = pltpu.get_barrier_semaphore()
    for d in range(1, n):
        peer = lax.rem(me + d, n)
        pl.semaphore_signal(barrier, inc=1, device_id=(peer, col), device_id_type=MESH)
    pl.semaphore_wait(barrier, n - 1)

    scatter = []
    for d in range(1, n):
        peer = lax.rem(me + d, n)
        start = pl.multiple_of(peer * chunk, chunk)
        copy = pltpu.make_async_remote_copy(
            src_ref=g_ref.at[pl.ds(start, chunk), :],
            dst_ref=recv.at[d],
            send_sem=send_sem.at[d],
            recv_sem=recv_sem.at[d],
            device_id=(peer, col),
            device_id_type=MESH,
        )
        copy.start()
        scatter.append(copy)

    mine = pl.multiple_of(me * chunk, chunk)
    total = g_ref[pl.ds(mine, chunk), :]
    for d in range(1, n):
        scatter[d - 1].wait_recv()
        total = total + recv[d]
    o_ref[pl.ds(mine, chunk), :] = total
    for copy in scatter:
        copy.wait_send()

    gather = []
    for d in range(1, n):
        peer = lax.rem(me + d, n)
        copy = pltpu.make_async_remote_copy(
            src_ref=o_ref.at[pl.ds(mine, chunk), :],
            dst_ref=o_ref.at[pl.ds(mine, chunk), :],
            send_sem=send2_sem.at[d],
            recv_sem=recv2_sem.at[d],
            device_id=(peer, col),
            device_id_type=MESH,
        )
        copy.start()
        gather.append(copy)
    for d in range(1, n):
        source = lax.rem(me + n - d, n)
        start = pl.multiple_of(source * chunk, chunk)
        pltpu.make_async_remote_copy(
            src_ref=o_ref.at[pl.ds(start, chunk), :],
            dst_ref=o_ref.at[pl.ds(start, chunk), :],
            send_sem=send2_sem.at[d],
            recv_sem=recv2_sem.at[d],
            device_id=(source, col),
            device_id_type=MESH,
        ).wait_recv()
    for copy in gather:
        copy.wait_send()


def allreduce_rows(g, key):
    n = lax.axis_size("rows")
    rows, cols = g.shape
    chunk = rows // n
    return pl.pallas_call(
        functools.partial(allreduce_kernel, n, chunk),
        out_shape=jax.ShapeDtypeStruct((rows, cols), g.dtype),
        in_specs=[pl.BlockSpec(memory_space=pltpu.VMEM)],
        out_specs=pl.BlockSpec(memory_space=pltpu.VMEM),
        scratch_shapes=[
            pltpu.VMEM((n, chunk, cols), g.dtype),
            pltpu.SemaphoreType.DMA((n,)),
            pltpu.SemaphoreType.DMA((n,)),
            pltpu.SemaphoreType.DMA((n,)),
            pltpu.SemaphoreType.DMA((n,)),
        ],
        compiler_params=pltpu.CompilerParams(collective_id=key, has_side_effects=True),
    )(g)


def eliminate(work, size):
    tile = 8
    lanes = 128
    for block in range(size // tile):
        top = block * tile
        low = (top // lanes) * lanes
        high = size + min(size, ((top + tile + lanes - 1) // lanes) * lanes)
        height = size - top
        here = (top // lanes) * lanes
        lane = lax.broadcasted_iota(jnp.int32, (1, lanes), 1) + here
        row_id = lax.broadcasted_iota(jnp.int32, (height, 1), 0) + top

        def step(t, carry, top=top, low=low, high=high, here=here, lane=lane, row_id=row_id):
            k = top + t
            row = work[pl.ds(k, 1), low:high]
            pivot = jnp.sum(jnp.where(lane == k, row[:, here - low:here - low + lanes], 0.0), axis=1, keepdims=True)
            scale = 1.0 / jnp.sqrt(pivot)
            pivot_row = row * scale
            column = jnp.sum(jnp.where(lane == k, work[top:, here:here + lanes], 0.0), axis=1, keepdims=True)
            column = jnp.where(row_id > k, column * scale, 0.0)
            work[top:, low:high] = work[top:, low:high] - column * pivot_row
            work[pl.ds(k, 1), low:high] = pivot_row
            return carry

        lax.fori_loop(0, tile, step, 0)


def inverse_kernel(a_ref, o_ref, work):
    size = a_ref.shape[0]
    half = size // 2
    rows_i = lax.broadcasted_iota(jnp.int32, (size, size), 0)
    cols_i = lax.broadcasted_iota(jnp.int32, (size, size), 1)
    diagonal = rows_i == cols_i
    a = a_ref[...]
    level = jnp.sum(jnp.where(diagonal, a, 0.0)) / size
    a = a + jnp.where(diagonal, 0.1 * level, 0.0)
    eye = jnp.where(diagonal[:half, :half], 1.0, 0.0).astype(a.dtype)
    hi = lax.Precision.HIGHEST
    nt = (((1,), (1,)), ((), ()))

    work[:, :half] = a[:half, :half]
    work[:, half:] = eye
    eliminate(work, half)
    inv11 = work[:, half:]
    low21 = lax.dot_general(a[half:, :half], inv11, nt, precision=hi, preferred_element_type=jnp.float32)
    schur = a[half:, half:] - lax.dot_general(low21, low21, nt, precision=hi, preferred_element_type=jnp.float32)
    work[:, :half] = schur
    work[:, half:] = eye
    eliminate(work, half)
    inv22 = work[:, half:]
    mid = jnp.dot(inv22, low21, precision=hi, preferred_element_type=jnp.float32)
    inv21 = -jnp.dot(mid, inv11, precision=hi, preferred_element_type=jnp.float32)
    o_ref[:half, :half] = inv11
    o_ref[:half, half:] = jnp.zeros((half, half), a.dtype)
    o_ref[half:, :half] = inv21
    o_ref[half:, half:] = inv22


def lower_inverse(scaled):
    size = scaled.shape[0]
    return pl.pallas_call(
        inverse_kernel,
        out_shape=jax.ShapeDtypeStruct((size, size), scaled.dtype),
        in_specs=[pl.BlockSpec(memory_space=pltpu.VMEM)],
        out_specs=pl.BlockSpec(memory_space=pltpu.VMEM),
        scratch_shapes=[pltpu.VMEM((size // 2, size), scaled.dtype)],
    )(scaled)


def whitener(scaled):
    return lower_inverse(scaled).T


def mm(left, right):
    return jnp.dot(left, right, precision=lax.Precision.HIGHEST)


def tmm(left, right):
    return gram_of(left, right)


def per_device(far, snapshots):
    local_rows = snapshots.shape[0]
    total = local_rows * lax.axis_size("rows")
    width = snapshots.shape[1] // 2
    count = lax.axis_size("pairs")
    index = lax.axis_index("pairs")
    first = index == 0
    last = index == count - 1
    pair = snapshots

    gram = allreduce_rows(gram_of(pair, pair), 0) / total
    sent, gram = lax.optimization_barrier((pair, gram))
    near_up = [(j, j + 1) for j in range(count - 1) if j not in far]
    near_down = [(j + 1, j) for j in range(count - 1) if j not in far]
    raw_a = jnp.where(first, pair, lax.ppermute(sent, "pairs", near_up))
    raw_b = jnp.where(last, pair, lax.ppermute(sent, "pairs", near_down))
    head = local_rows // 2
    far_up = [(j, j + 1) for j in sorted(far)]
    far_down = [(j + 1, j) for j in sorted(far)]
    if far:
        head_a = lax.ppermute(sent[:head], "pairs", far_up)
        head_b = lax.ppermute(sent[:head], "pairs", far_down)

    whiten = whitener(gram)
    moment = tmm(whiten, mm(gram, whiten))
    top = jnp.concatenate([whiten[:, :width], moment[:width, :width]], axis=0)
    bottom = jnp.concatenate([whiten[:, width:], moment[width:, width:]], axis=0)
    outgoing = jnp.where(first, bottom, top)
    rows = whiten.shape[0]
    if far:
        up = jnp.concatenate([outgoing, mm(pair[head:], outgoing[:rows])], axis=0)
        down = jnp.concatenate([bottom, mm(pair[head:], bottom[:rows])], axis=0)
    else:
        up, down = outgoing, bottom
    arrived_a = from_behind(up, "pairs", 1)
    arrived_b = from_behind(down, "pairs", -1)
    info = top.shape[0]
    side_a = jnp.where(first, top, arrived_a[:info])
    side_b = jnp.where(last, top, arrived_b[:info])
    x_a, m_a = side_a[:rows], side_a[rows:]
    x_b, m_b = side_b[:rows], side_b[rows:]

    top_next = mm(raw_a, x_a)
    bottom_next = mm(raw_b, x_b)
    if far:
        far_a = jnp.asarray([j - 1 in far for j in range(count)])[index]
        far_b = jnp.asarray([j in far for j in range(count)])[index]
        split_a = jnp.concatenate([mm(head_a, x_a), arrived_a[info:]], axis=0)
        split_b = jnp.concatenate([mm(head_b, x_b), arrived_b[info:]], axis=0)
        top_next = jnp.where(far_a, split_a, top_next)
        bottom_next = jnp.where(far_b, split_b, bottom_next)

    off = allreduce_rows(gram_of(top_next, bottom_next), 1) / total
    gram2 = jnp.concatenate(
        [jnp.concatenate([m_a, off], axis=1), jnp.concatenate([off.T, m_b], axis=1)], axis=0
    )
    whiten2 = whitener(gram2)
    return mm(top_next, whiten2[:width]) + mm(bottom_next, whiten2[width:])


def far_links(mesh):
    far = set()
    line = mesh.devices[0]
    for j in range(len(line) - 1):
        here, there = getattr(line[j], "coords", None), getattr(line[j + 1], "coords", None)
        if here is None or there is None:
            continue
        gaps = [abs(p - q) for p, q in zip(here, there)]
        if sum(gaps) > 1:
            far.add(j)
    return frozenset(far)


def solution(mesh):
    return jax.shard_map(
        functools.partial(per_device, far_links(mesh)),
        mesh=mesh,
        in_specs=(P("rows", "pairs"),),
        out_specs=P("rows", "pairs"),
        check_vma=False,
    )
```

```python
import functools

import jax
import jax.numpy as jnp
from jax import lax
from jax.experimental import pallas as pl
from jax.experimental.pallas import tpu as pltpu
from jax.sharding import PartitionSpec as P

MESH = pl.DeviceIdType.MESH


def from_behind(value, axis, steps):
    count = lax.axis_size(axis)
    leading, last = (max(0, -steps), min(count, count - steps))
    return lax.ppermute(value, axis, [(source, source + steps) for source in range(leading, last)])


def gram_of(left, right):
    return lax.dot_general(left, right, (((0,), (0,)), ((), ())), precision=lax.Precision.HIGHEST)


def allreduce_kernel(n, chunk, g_ref, o_ref, recv, send_sem, recv_sem, send2_sem, recv2_sem):
    me = lax.axis_index("rows")
    col = lax.axis_index("pairs")

    barrier = pltpu.get_barrier_semaphore()
    for d in range(1, n):
        peer = lax.rem(me + d, n)
        pl.semaphore_signal(barrier, inc=1, device_id=(peer, col), device_id_type=MESH)
    pl.semaphore_wait(barrier, n - 1)

    scatter = []
    for d in range(1, n):
        peer = lax.rem(me + d, n)
        start = pl.multiple_of(peer * chunk, chunk)
        copy = pltpu.make_async_remote_copy(
            src_ref=g_ref.at[pl.ds(start, chunk), :],
            dst_ref=recv.at[d],
            send_sem=send_sem.at[d],
            recv_sem=recv_sem.at[d],
            device_id=(peer, col),
            device_id_type=MESH,
        )
        copy.start()
        scatter.append(copy)

    mine = pl.multiple_of(me * chunk, chunk)
    total = g_ref[pl.ds(mine, chunk), :]
    for d in range(1, n):
        scatter[d - 1].wait_recv()
        total = total + recv[d]
    o_ref[pl.ds(mine, chunk), :] = total
    for copy in scatter:
        copy.wait_send()

    gather = []
    for d in range(1, n):
        peer = lax.rem(me + d, n)
        copy = pltpu.make_async_remote_copy(
            src_ref=o_ref.at[pl.ds(mine, chunk), :],
            dst_ref=o_ref.at[pl.ds(mine, chunk), :],
            send_sem=send2_sem.at[d],
            recv_sem=recv2_sem.at[d],
            device_id=(peer, col),
            device_id_type=MESH,
        )
        copy.start()
        gather.append(copy)
    for d in range(1, n):
        source = lax.rem(me + n - d, n)
        start = pl.multiple_of(source * chunk, chunk)
        pltpu.make_async_remote_copy(
            src_ref=o_ref.at[pl.ds(start, chunk), :],
            dst_ref=o_ref.at[pl.ds(start, chunk), :],
            send_sem=send2_sem.at[d],
            recv_sem=recv2_sem.at[d],
            device_id=(source, col),
            device_id_type=MESH,
        ).wait_recv()
    for copy in gather:
        copy.wait_send()


def allreduce_rows(g):
    n = lax.axis_size("rows")
    rows, cols = g.shape
    chunk = rows // n
    return pl.pallas_call(
        functools.partial(allreduce_kernel, n, chunk),
        out_shape=jax.ShapeDtypeStruct((rows, cols), g.dtype),
        in_specs=[pl.BlockSpec(memory_space=pltpu.VMEM)],
        out_specs=pl.BlockSpec(memory_space=pltpu.VMEM),
        scratch_shapes=[
            pltpu.VMEM((n, chunk, cols), g.dtype),
            pltpu.SemaphoreType.DMA((n,)),
            pltpu.SemaphoreType.DMA((n,)),
            pltpu.SemaphoreType.DMA((n,)),
            pltpu.SemaphoreType.DMA((n,)),
        ],
        compiler_params=pltpu.CompilerParams(collective_id=0, has_side_effects=True),
    )(g)


def eliminate(work, size):
    tile = 8
    lanes = 128
    for block in range(size // tile):
        top = block * tile
        low = (top // lanes) * lanes
        high = size + min(size, ((top + tile + lanes - 1) // lanes) * lanes)
        height = size - top
        here = (top // lanes) * lanes
        lane = lax.broadcasted_iota(jnp.int32, (1, lanes), 1) + here
        row_id = lax.broadcasted_iota(jnp.int32, (height, 1), 0) + top

        def step(t, carry, top=top, low=low, high=high, here=here, lane=lane, row_id=row_id):
            k = top + t
            row = work[pl.ds(k, 1), low:high]
            pivot = jnp.sum(jnp.where(lane == k, row[:, here - low:here - low + lanes], 0.0), axis=1, keepdims=True)
            scale = lax.rsqrt(pivot)
            pivot_row = row * scale
            column = jnp.sum(jnp.where(lane == k, work[top:, here:here + lanes], 0.0), axis=1, keepdims=True)
            column = jnp.where(row_id > k, column * scale, 0.0)
            work[top:, low:high] = work[top:, low:high] - column * pivot_row
            work[pl.ds(k, 1), low:high] = pivot_row
            return carry

        lax.fori_loop(0, tile, step, 0)


def inverse_kernel(a_ref, o_ref, work):
    size = a_ref.shape[0]
    half = size // 2
    rows_i = lax.broadcasted_iota(jnp.int32, (size, size), 0)
    cols_i = lax.broadcasted_iota(jnp.int32, (size, size), 1)
    diagonal = rows_i == cols_i
    a = a_ref[...]
    level = jnp.sum(jnp.where(diagonal, a, 0.0)) / size
    a = a + jnp.where(diagonal, 0.1 * level, 0.0)
    eye = jnp.where(diagonal[:half, :half], 1.0, 0.0).astype(a.dtype)
    hi = lax.Precision.HIGHEST
    nt = (((1,), (1,)), ((), ()))

    work[:, :half] = a[:half, :half]
    work[:, half:] = eye
    eliminate(work, half)
    inv11 = work[:, half:]
    low21 = lax.dot_general(a[half:, :half], inv11, nt, precision=hi, preferred_element_type=jnp.float32)
    schur = a[half:, half:] - lax.dot_general(low21, low21, nt, precision=hi, preferred_element_type=jnp.float32)
    work[:, :half] = schur
    work[:, half:] = eye
    eliminate(work, half)
    inv22 = work[:, half:]
    mid = jnp.dot(inv22, low21, precision=hi, preferred_element_type=jnp.float32)
    inv21 = -jnp.dot(mid, inv11, precision=hi, preferred_element_type=jnp.float32)
    o_ref[:half, :half] = inv11
    o_ref[:half, half:] = jnp.zeros((half, half), a.dtype)
    o_ref[half:, :half] = inv21
    o_ref[half:, half:] = inv22


def lower_inverse(scaled):
    size = scaled.shape[0]
    return pl.pallas_call(
        inverse_kernel,
        out_shape=jax.ShapeDtypeStruct((size, size), scaled.dtype),
        in_specs=[pl.BlockSpec(memory_space=pltpu.VMEM)],
        out_specs=pl.BlockSpec(memory_space=pltpu.VMEM),
        scratch_shapes=[pltpu.VMEM((size // 2, size), scaled.dtype)],
    )(scaled)


def whitener(scaled):
    return lower_inverse(scaled).T


def mm(left, right):
    return jnp.dot(left, right, precision=lax.Precision.HIGHEST)


def tmm(left, right):
    return gram_of(left, right)


def per_device(snapshots):
    local_rows = snapshots.shape[0]
    total = local_rows * lax.axis_size("rows")
    width = snapshots.shape[1] // 2
    count = lax.axis_size("pairs")
    index = lax.axis_index("pairs")
    first = index == 0
    last = index == count - 1
    pair = snapshots

    gram = allreduce_rows(gram_of(pair, pair)) / total
    sent, gram = lax.optimization_barrier((pair, gram))
    raw_a = jnp.where(first, pair, from_behind(sent, "pairs", 1))
    raw_b = jnp.where(last, pair, from_behind(sent, "pairs", -1))

    cross = allreduce_rows(gram_of(raw_a, raw_b)) / total

    whiten = whitener(gram)
    moment = tmm(whiten, mm(gram, whiten))
    top = jnp.concatenate([whiten[:, :width], moment[:width, :width]], axis=0)
    bottom = jnp.concatenate([whiten[:, width:], moment[width:, width:]], axis=0)
    outgoing = jnp.where(first, bottom, top)
    arrived_a = from_behind(outgoing, "pairs", 1)
    arrived_b = from_behind(bottom, "pairs", -1)
    side_a = jnp.where(first, top, arrived_a)
    side_b = jnp.where(last, top, arrived_b)
    rows = whiten.shape[0]
    x_a, m_a = side_a[:rows], side_a[rows:]
    x_b, m_b = side_b[:rows], side_b[rows:]

    off = tmm(x_a, mm(cross, x_b))
    gram2 = jnp.concatenate(
        [jnp.concatenate([m_a, off], axis=1), jnp.concatenate([off.T, m_b], axis=1)], axis=0
    )
    whiten2 = whitener(gram2)
    combined = jnp.concatenate([mm(x_a, whiten2[:width]), mm(x_b, whiten2[width:])], axis=0)
    return mm(jnp.concatenate([raw_a, raw_b], axis=1), combined)


def solution(mesh):
    return jax.shard_map(
        per_device,
        mesh=mesh,
        in_specs=(P("rows", "pairs"),),
        out_specs=P("rows", "pairs"),
        check_vma=False,
    )
```

```python
import functools

import jax
import jax.numpy as jnp
from jax import lax
from jax.experimental import pallas as pl
from jax.experimental.pallas import tpu as pltpu
from jax.sharding import PartitionSpec as P

MESH = pl.DeviceIdType.MESH


def from_behind(value, axis, steps):
    count = lax.axis_size(axis)
    leading, last = (max(0, -steps), min(count, count - steps))
    return lax.ppermute(value, axis, [(source, source + steps) for source in range(leading, last)])


def gram_of(left, right):
    return lax.dot_general(left, right, (((0,), (0,)), ((), ())), precision=lax.Precision.HIGHEST)


def allreduce_kernel(n, chunk, g_ref, o_ref, recv, send_sem, recv_sem, send2_sem, recv2_sem):
    me = lax.axis_index("rows")
    col = lax.axis_index("pairs")

    barrier = pltpu.get_barrier_semaphore()
    for d in range(1, n):
        peer = lax.rem(me + d, n)
        pl.semaphore_signal(barrier, inc=1, device_id=(peer, col), device_id_type=MESH)
    pl.semaphore_wait(barrier, n - 1)

    scatter = []
    for d in range(1, n):
        peer = lax.rem(me + d, n)
        start = pl.multiple_of(peer * chunk, chunk)
        copy = pltpu.make_async_remote_copy(
            src_ref=g_ref.at[pl.ds(start, chunk), :],
            dst_ref=recv.at[d],
            send_sem=send_sem.at[d],
            recv_sem=recv_sem.at[d],
            device_id=(peer, col),
            device_id_type=MESH,
        )
        copy.start()
        scatter.append(copy)

    mine = pl.multiple_of(me * chunk, chunk)
    total = g_ref[pl.ds(mine, chunk), :]
    for d in range(1, n):
        scatter[d - 1].wait_recv()
        total = total + recv[d]
    o_ref[pl.ds(mine, chunk), :] = total
    for copy in scatter:
        copy.wait_send()

    gather = []
    for d in range(1, n):
        peer = lax.rem(me + d, n)
        copy = pltpu.make_async_remote_copy(
            src_ref=o_ref.at[pl.ds(mine, chunk), :],
            dst_ref=o_ref.at[pl.ds(mine, chunk), :],
            send_sem=send2_sem.at[d],
            recv_sem=recv2_sem.at[d],
            device_id=(peer, col),
            device_id_type=MESH,
        )
        copy.start()
        gather.append(copy)
    for d in range(1, n):
        source = lax.rem(me + n - d, n)
        start = pl.multiple_of(source * chunk, chunk)
        pltpu.make_async_remote_copy(
            src_ref=o_ref.at[pl.ds(start, chunk), :],
            dst_ref=o_ref.at[pl.ds(start, chunk), :],
            send_sem=send2_sem.at[d],
            recv_sem=recv2_sem.at[d],
            device_id=(source, col),
            device_id_type=MESH,
        ).wait_recv()
    for copy in gather:
        copy.wait_send()


def allreduce_rows(g, key=0):
    n = lax.axis_size("rows")
    rows, cols = g.shape
    chunk = rows // n
    return pl.pallas_call(
        functools.partial(allreduce_kernel, n, chunk),
        out_shape=jax.ShapeDtypeStruct((rows, cols), g.dtype),
        in_specs=[pl.BlockSpec(memory_space=pltpu.VMEM)],
        out_specs=pl.BlockSpec(memory_space=pltpu.VMEM),
        scratch_shapes=[
            pltpu.VMEM((n, chunk, cols), g.dtype),
            pltpu.SemaphoreType.DMA((n,)),
            pltpu.SemaphoreType.DMA((n,)),
            pltpu.SemaphoreType.DMA((n,)),
            pltpu.SemaphoreType.DMA((n,)),
        ],
        compiler_params=pltpu.CompilerParams(collective_id=key, has_side_effects=True),
    )(g)


def eliminate(work, size):
    tile = 8
    lanes = 128
    for block in range(size // tile):
        top = block * tile
        low = (top // lanes) * lanes
        high = size + min(size, ((top + tile + lanes - 1) // lanes) * lanes)
        height = size - top
        here = (top // lanes) * lanes
        lane = lax.broadcasted_iota(jnp.int32, (1, lanes), 1) + here
        row_id = lax.broadcasted_iota(jnp.int32, (height, 1), 0) + top

        def step(t, carry, top=top, low=low, high=high, here=here, lane=lane, row_id=row_id):
            k = top + t
            row = work[pl.ds(k, 1), low:high]
            pivot = jnp.sum(jnp.where(lane == k, row[:, here - low:here - low + lanes], 0.0), axis=1, keepdims=True)
            scale = lax.rsqrt(pivot)
            pivot_row = row * scale
            column = jnp.sum(jnp.where(lane == k, work[top:, here:here + lanes], 0.0), axis=1, keepdims=True)
            column = jnp.where(row_id > k, column * scale, 0.0)
            work[top:, low:high] = work[top:, low:high] - column * pivot_row
            work[pl.ds(k, 1), low:high] = pivot_row
            return carry

        lax.fori_loop(0, tile, step, 0)


def inverse_kernel(a_ref, o_ref, work):
    size = a_ref.shape[0]
    half = size // 2
    rows_i = lax.broadcasted_iota(jnp.int32, (size, size), 0)
    cols_i = lax.broadcasted_iota(jnp.int32, (size, size), 1)
    diagonal = rows_i == cols_i
    a = a_ref[...]
    level = jnp.sum(jnp.where(diagonal, a, 0.0)) / size
    a = a + jnp.where(diagonal, 0.1 * level, 0.0)
    eye = jnp.where(diagonal[:half, :half], 1.0, 0.0).astype(a.dtype)
    hi = lax.Precision.HIGHEST
    nt = (((1,), (1,)), ((), ()))

    work[:, :half] = a[:half, :half]
    work[:, half:] = eye
    eliminate(work, half)
    inv11 = work[:, half:]
    low21 = lax.dot_general(a[half:, :half], inv11, nt, precision=hi, preferred_element_type=jnp.float32)
    schur = a[half:, half:] - lax.dot_general(low21, low21, nt, precision=hi, preferred_element_type=jnp.float32)
    work[:, :half] = schur
    work[:, half:] = eye
    eliminate(work, half)
    inv22 = work[:, half:]
    mid = jnp.dot(inv22, low21, precision=hi, preferred_element_type=jnp.float32)
    inv21 = -jnp.dot(mid, inv11, precision=hi, preferred_element_type=jnp.float32)
    o_ref[:half, :half] = inv11
    o_ref[:half, half:] = jnp.zeros((half, half), a.dtype)
    o_ref[half:, :half] = inv21
    o_ref[half:, half:] = inv22


def lower_inverse(scaled):
    size = scaled.shape[0]
    return pl.pallas_call(
        inverse_kernel,
        out_shape=jax.ShapeDtypeStruct((size, size), scaled.dtype),
        in_specs=[pl.BlockSpec(memory_space=pltpu.VMEM)],
        out_specs=pl.BlockSpec(memory_space=pltpu.VMEM),
        scratch_shapes=[pltpu.VMEM((size // 2, size), scaled.dtype)],
    )(scaled)


def whitener(scaled):
    return lower_inverse(scaled).T


def mm(left, right):
    return jnp.dot(left, right, precision=lax.Precision.HIGHEST)


def tmm(left, right):
    return gram_of(left, right)


def per_device(snapshots):
    local_rows = snapshots.shape[0]
    total = local_rows * lax.axis_size("rows")
    width = snapshots.shape[1] // 2
    count = lax.axis_size("pairs")
    index = lax.axis_index("pairs")
    first = index == 0
    last = index == count - 1
    pair = snapshots

    gram = allreduce_rows(gram_of(pair, pair)) / total
    sent, gram = lax.optimization_barrier((pair, gram))
    raw_a = jnp.where(first, pair, from_behind(sent, "pairs", 1))
    raw_b = jnp.where(last, pair, from_behind(sent, "pairs", -1))


    whiten = whitener(gram)
    moment = tmm(whiten, mm(gram, whiten))
    top = jnp.concatenate([whiten[:, :width], moment[:width, :width]], axis=0)
    bottom = jnp.concatenate([whiten[:, width:], moment[width:, width:]], axis=0)
    outgoing = jnp.where(first, bottom, top)
    arrived_a = from_behind(outgoing, "pairs", 1)
    arrived_b = from_behind(bottom, "pairs", -1)
    side_a = jnp.where(first, top, arrived_a)
    side_b = jnp.where(last, top, arrived_b)
    rows = whiten.shape[0]
    x_a, m_a = side_a[:rows], side_a[rows:]
    x_b, m_b = side_b[:rows], side_b[rows:]

    off = allreduce_rows(tmm(x_a, mm(gram_of(raw_a, raw_b), x_b)), 1) / total
    gram2 = jnp.concatenate(
        [jnp.concatenate([m_a, off], axis=1), jnp.concatenate([off.T, m_b], axis=1)], axis=0
    )
    whiten2 = whitener(gram2)
    combined = jnp.concatenate([mm(x_a, whiten2[:width]), mm(x_b, whiten2[width:])], axis=0)
    return mm(jnp.concatenate([raw_a, raw_b], axis=1), combined)


def solution(mesh):
    return jax.shard_map(
        per_device,
        mesh=mesh,
        in_specs=(P("rows", "pairs"),),
        out_specs=P("rows", "pairs"),
        check_vma=False,
    )
```

```python
import functools

import jax
import jax.numpy as jnp
from jax import lax
from jax.experimental import pallas as pl
from jax.experimental.pallas import tpu as pltpu
from jax.sharding import PartitionSpec as P

MESH = pl.DeviceIdType.MESH


def from_behind(value, axis, steps):
    count = lax.axis_size(axis)
    leading, last = (max(0, -steps), min(count, count - steps))
    return lax.ppermute(value, axis, [(source, source + steps) for source in range(leading, last)])


def gram_of(left, right):
    return lax.dot_general(left, right, (((0,), (0,)), ((), ())), precision=lax.Precision.HIGHEST)


def allreduce_kernel(n, chunk, g_ref, o_ref, recv, send_sem, recv_sem, send2_sem, recv2_sem):
    me = lax.axis_index("rows")
    col = lax.axis_index("pairs")

    barrier = pltpu.get_barrier_semaphore()
    for d in range(1, n):
        peer = lax.rem(me + d, n)
        pl.semaphore_signal(barrier, inc=1, device_id=(peer, col), device_id_type=MESH)
    pl.semaphore_wait(barrier, n - 1)

    scatter = []
    for d in range(1, n):
        peer = lax.rem(me + d, n)
        start = pl.multiple_of(peer * chunk, chunk)
        copy = pltpu.make_async_remote_copy(
            src_ref=g_ref.at[pl.ds(start, chunk), :],
            dst_ref=recv.at[d],
            send_sem=send_sem.at[d],
            recv_sem=recv_sem.at[d],
            device_id=(peer, col),
            device_id_type=MESH,
        )
        copy.start()
        scatter.append(copy)

    mine = pl.multiple_of(me * chunk, chunk)
    total = g_ref[pl.ds(mine, chunk), :]
    for d in range(1, n):
        scatter[d - 1].wait_recv()
        total = total + recv[d]
    o_ref[pl.ds(mine, chunk), :] = total
    for copy in scatter:
        copy.wait_send()

    gather = []
    for d in range(1, n):
        peer = lax.rem(me + d, n)
        copy = pltpu.make_async_remote_copy(
            src_ref=o_ref.at[pl.ds(mine, chunk), :],
            dst_ref=o_ref.at[pl.ds(mine, chunk), :],
            send_sem=send2_sem.at[d],
            recv_sem=recv2_sem.at[d],
            device_id=(peer, col),
            device_id_type=MESH,
        )
        copy.start()
        gather.append(copy)
    for d in range(1, n):
        source = lax.rem(me + n - d, n)
        start = pl.multiple_of(source * chunk, chunk)
        pltpu.make_async_remote_copy(
            src_ref=o_ref.at[pl.ds(start, chunk), :],
            dst_ref=o_ref.at[pl.ds(start, chunk), :],
            send_sem=send2_sem.at[d],
            recv_sem=recv2_sem.at[d],
            device_id=(source, col),
            device_id_type=MESH,
        ).wait_recv()
    for copy in gather:
        copy.wait_send()


def allreduce_rows(g, key=0):
    n = lax.axis_size("rows")
    rows, cols = g.shape
    chunk = rows // n
    return pl.pallas_call(
        functools.partial(allreduce_kernel, n, chunk),
        out_shape=jax.ShapeDtypeStruct((rows, cols), g.dtype),
        in_specs=[pl.BlockSpec(memory_space=pltpu.VMEM)],
        out_specs=pl.BlockSpec(memory_space=pltpu.VMEM),
        scratch_shapes=[
            pltpu.VMEM((n, chunk, cols), g.dtype),
            pltpu.SemaphoreType.DMA((n,)),
            pltpu.SemaphoreType.DMA((n,)),
            pltpu.SemaphoreType.DMA((n,)),
            pltpu.SemaphoreType.DMA((n,)),
        ],
        compiler_params=pltpu.CompilerParams(collective_id=key, has_side_effects=True),
    )(g)


def eliminate(work, size):
    tile = 8
    lanes = 128
    for block in range(size // tile):
        top = block * tile
        low = (top // lanes) * lanes
        high = size + min(size, ((top + tile + lanes - 1) // lanes) * lanes)
        height = size - top
        here = (top // lanes) * lanes
        lane = lax.broadcasted_iota(jnp.int32, (1, lanes), 1) + here
        row_id = lax.broadcasted_iota(jnp.int32, (height, 1), 0) + top

        def step(t, carry, top=top, low=low, high=high, here=here, lane=lane, row_id=row_id):
            k = top + t
            row = work[pl.ds(k, 1), low:high]
            pivot = jnp.sum(jnp.where(lane == k, row[:, here - low:here - low + lanes], 0.0), axis=1, keepdims=True)
            scale = lax.rsqrt(pivot)
            pivot_row = row * scale
            column = jnp.sum(jnp.where(lane == k, work[top:, here:here + lanes], 0.0), axis=1, keepdims=True)
            column = jnp.where(row_id > k, column * scale, 0.0)
            work[top:, low:high] = work[top:, low:high] - column * pivot_row
            work[pl.ds(k, 1), low:high] = pivot_row
            return carry

        lax.fori_loop(0, tile, step, 0)


def inverse_kernel(a_ref, o_ref, work):
    size = a_ref.shape[0]
    half = size // 2
    rows_i = lax.broadcasted_iota(jnp.int32, (size, size), 0)
    cols_i = lax.broadcasted_iota(jnp.int32, (size, size), 1)
    diagonal = rows_i == cols_i
    a = a_ref[...]
    level = jnp.sum(jnp.where(diagonal, a, 0.0)) / size
    a = a + jnp.where(diagonal, 0.1 * level, 0.0)
    eye = jnp.where(diagonal[:half, :half], 1.0, 0.0).astype(a.dtype)
    hi = lax.Precision.HIGHEST
    nt = (((1,), (1,)), ((), ()))

    work[:, :half] = a[:half, :half]
    work[:, half:] = eye
    eliminate(work, half)
    inv11 = work[:, half:]
    low21 = lax.dot_general(a[half:, :half], inv11, nt, precision=hi, preferred_element_type=jnp.float32)
    schur = a[half:, half:] - lax.dot_general(low21, low21, nt, precision=hi, preferred_element_type=jnp.float32)
    work[:, :half] = schur
    work[:, half:] = eye
    eliminate(work, half)
    inv22 = work[:, half:]
    mid = jnp.dot(inv22, low21, precision=hi, preferred_element_type=jnp.float32)
    inv21 = -jnp.dot(mid, inv11, precision=hi, preferred_element_type=jnp.float32)
    o_ref[:half, :half] = inv11
    o_ref[:half, half:] = jnp.zeros((half, half), a.dtype)
    o_ref[half:, :half] = inv21
    o_ref[half:, half:] = inv22


def head_kernel(a_ref, o_ref, work):
    half = a_ref.shape[0]
    rows_i = lax.broadcasted_iota(jnp.int32, (half, half), 0)
    cols_i = lax.broadcasted_iota(jnp.int32, (half, half), 1)
    work[:, :half] = a_ref[...]
    work[:, half:] = jnp.where(rows_i == cols_i, 1.0, 0.0).astype(work.dtype)
    eliminate(work, half)
    o_ref[...] = work[:, half:]


def tail_kernel(a21_ref, inv11_ref, a22_ref, o_ref, work):
    half = a22_ref.shape[0]
    rows_i = lax.broadcasted_iota(jnp.int32, (half, half), 0)
    cols_i = lax.broadcasted_iota(jnp.int32, (half, half), 1)
    hi = lax.Precision.HIGHEST
    nt = (((1,), (1,)), ((), ()))
    inv11 = inv11_ref[...]
    low21 = lax.dot_general(a21_ref[...], inv11, nt, precision=hi, preferred_element_type=jnp.float32)
    schur = a22_ref[...] - lax.dot_general(low21, low21, nt, precision=hi, preferred_element_type=jnp.float32)
    work[:, :half] = schur
    work[:, half:] = jnp.where(rows_i == cols_i, 1.0, 0.0).astype(work.dtype)
    eliminate(work, half)
    inv22 = work[:, half:]
    mid = jnp.dot(inv22, low21, precision=hi, preferred_element_type=jnp.float32)
    o_ref[:half, :half] = inv11
    o_ref[:half, half:] = jnp.zeros((half, half), inv11.dtype)
    o_ref[half:, :half] = -jnp.dot(mid, inv11, precision=hi, preferred_element_type=jnp.float32)
    o_ref[half:, half:] = inv22


def head_inverse(a11):
    half = a11.shape[0]
    return pl.pallas_call(
        head_kernel,
        out_shape=jax.ShapeDtypeStruct((half, half), a11.dtype),
        in_specs=[pl.BlockSpec(memory_space=pltpu.VMEM)],
        out_specs=pl.BlockSpec(memory_space=pltpu.VMEM),
        scratch_shapes=[pltpu.VMEM((half, 2 * half), a11.dtype)],
    )(a11)


def tail_inverse(a21, inv11, a22):
    half = a22.shape[0]
    return pl.pallas_call(
        tail_kernel,
        out_shape=jax.ShapeDtypeStruct((2 * half, 2 * half), a22.dtype),
        in_specs=[pl.BlockSpec(memory_space=pltpu.VMEM)] * 3,
        out_specs=pl.BlockSpec(memory_space=pltpu.VMEM),
        scratch_shapes=[pltpu.VMEM((half, 2 * half), a22.dtype)],
    )(a21, inv11, a22)


def lower_inverse(scaled):
    size = scaled.shape[0]
    return pl.pallas_call(
        inverse_kernel,
        out_shape=jax.ShapeDtypeStruct((size, size), scaled.dtype),
        in_specs=[pl.BlockSpec(memory_space=pltpu.VMEM)],
        out_specs=pl.BlockSpec(memory_space=pltpu.VMEM),
        scratch_shapes=[pltpu.VMEM((size // 2, size), scaled.dtype)],
    )(scaled)


def whitener(scaled):
    return lower_inverse(scaled).T


def mm(left, right):
    return jnp.dot(left, right, precision=lax.Precision.HIGHEST)


def tmm(left, right):
    return gram_of(left, right)


def per_device(snapshots):
    local_rows = snapshots.shape[0]
    total = local_rows * lax.axis_size("rows")
    width = snapshots.shape[1] // 2
    count = lax.axis_size("pairs")
    index = lax.axis_index("pairs")
    first = index == 0
    last = index == count - 1
    pair = snapshots

    gram = allreduce_rows(gram_of(pair, pair)) / total
    sent, gram = lax.optimization_barrier((pair, gram))
    raw_a = jnp.where(first, pair, from_behind(sent, "pairs", 1))
    raw_b = jnp.where(last, pair, from_behind(sent, "pairs", -1))


    whiten = whitener(gram)
    moment = tmm(whiten, mm(gram, whiten))
    top = jnp.concatenate([whiten[:, :width], moment[:width, :width]], axis=0)
    bottom = jnp.concatenate([whiten[:, width:], moment[width:, width:]], axis=0)
    outgoing = jnp.where(first, bottom, top)
    arrived_a = from_behind(outgoing, "pairs", 1)
    arrived_b = from_behind(bottom, "pairs", -1)
    side_a = jnp.where(first, top, arrived_a)
    side_b = jnp.where(last, top, arrived_b)
    rows = whiten.shape[0]
    x_a, m_a = side_a[:rows], side_a[rows:]
    x_b, m_b = side_b[:rows], side_b[rows:]

    level = (jnp.trace(m_a) + jnp.trace(m_b)) / (2 * width)
    shift = 0.1 * level * jnp.eye(width, dtype=m_a.dtype)
    inv11 = head_inverse(m_a + shift)
    off = allreduce_rows(tmm(x_a, mm(gram_of(raw_a, raw_b), x_b)), 1) / total
    whiten2 = tail_inverse(off.T, inv11, m_b + shift).T
    combined = jnp.concatenate([mm(x_a, whiten2[:width]), mm(x_b, whiten2[width:])], axis=0)
    return mm(jnp.concatenate([raw_a, raw_b], axis=1), combined)


def solution(mesh):
    return jax.shard_map(
        per_device,
        mesh=mesh,
        in_specs=(P("rows", "pairs"),),
        out_specs=P("rows", "pairs"),
        check_vma=False,
    )
```

```python
import functools

import jax
import jax.numpy as jnp
from jax import lax
from jax.experimental import pallas as pl
from jax.experimental.pallas import tpu as pltpu
from jax.sharding import PartitionSpec as P

MESH = pl.DeviceIdType.MESH


def from_behind(value, axis, steps):
    count = lax.axis_size(axis)
    leading, last = (max(0, -steps), min(count, count - steps))
    return lax.ppermute(value, axis, [(source, source + steps) for source in range(leading, last)])


def gram_of(left, right):
    return lax.dot_general(left, right, (((0,), (0,)), ((), ())), precision=lax.Precision.HIGHEST)


def allreduce_kernel(n, chunk, g_ref, o_ref, recv, send_sem, recv_sem, send2_sem, recv2_sem):
    me = lax.axis_index("rows")
    col = lax.axis_index("pairs")

    barrier = pltpu.get_barrier_semaphore()
    for d in range(1, n):
        peer = lax.rem(me + d, n)
        pl.semaphore_signal(barrier, inc=1, device_id=(peer, col), device_id_type=MESH)
    pl.semaphore_wait(barrier, n - 1)

    scatter = []
    for d in range(1, n):
        peer = lax.rem(me + d, n)
        start = pl.multiple_of(peer * chunk, chunk)
        copy = pltpu.make_async_remote_copy(
            src_ref=g_ref.at[pl.ds(start, chunk), :],
            dst_ref=recv.at[d],
            send_sem=send_sem.at[d],
            recv_sem=recv_sem.at[d],
            device_id=(peer, col),
            device_id_type=MESH,
        )
        copy.start()
        scatter.append(copy)

    mine = pl.multiple_of(me * chunk, chunk)
    total = g_ref[pl.ds(mine, chunk), :]
    for d in range(1, n):
        scatter[d - 1].wait_recv()
        total = total + recv[d]
    o_ref[pl.ds(mine, chunk), :] = total
    for copy in scatter:
        copy.wait_send()

    gather = []
    for d in range(1, n):
        peer = lax.rem(me + d, n)
        copy = pltpu.make_async_remote_copy(
            src_ref=o_ref.at[pl.ds(mine, chunk), :],
            dst_ref=o_ref.at[pl.ds(mine, chunk), :],
            send_sem=send2_sem.at[d],
            recv_sem=recv2_sem.at[d],
            device_id=(peer, col),
            device_id_type=MESH,
        )
        copy.start()
        gather.append(copy)
    for d in range(1, n):
        source = lax.rem(me + n - d, n)
        start = pl.multiple_of(source * chunk, chunk)
        pltpu.make_async_remote_copy(
            src_ref=o_ref.at[pl.ds(start, chunk), :],
            dst_ref=o_ref.at[pl.ds(start, chunk), :],
            send_sem=send2_sem.at[d],
            recv_sem=recv2_sem.at[d],
            device_id=(source, col),
            device_id_type=MESH,
        ).wait_recv()
    for copy in gather:
        copy.wait_send()


def allreduce_rows(g, key=0):
    n = lax.axis_size("rows")
    rows, cols = g.shape
    chunk = rows // n
    return pl.pallas_call(
        functools.partial(allreduce_kernel, n, chunk),
        out_shape=jax.ShapeDtypeStruct((rows, cols), g.dtype),
        in_specs=[pl.BlockSpec(memory_space=pltpu.VMEM)],
        out_specs=pl.BlockSpec(memory_space=pltpu.VMEM),
        scratch_shapes=[
            pltpu.VMEM((n, chunk, cols), g.dtype),
            pltpu.SemaphoreType.DMA((n,)),
            pltpu.SemaphoreType.DMA((n,)),
            pltpu.SemaphoreType.DMA((n,)),
            pltpu.SemaphoreType.DMA((n,)),
        ],
        compiler_params=pltpu.CompilerParams(collective_id=key, has_side_effects=True),
    )(g)


def eliminate(work, size):
    tile = 8
    lanes = 128
    for block in range(size // tile):
        top = block * tile
        low = (top // lanes) * lanes
        high = size + min(size, ((top + tile + lanes - 1) // lanes) * lanes)
        height = size - top
        here = (top // lanes) * lanes
        lane = lax.broadcasted_iota(jnp.int32, (1, lanes), 1) + here
        row_id = lax.broadcasted_iota(jnp.int32, (height, 1), 0) + top

        def step(t, carry, top=top, low=low, high=high, here=here, lane=lane, row_id=row_id):
            k = top + t
            row = work[pl.ds(k, 1), low:high]
            pivot = jnp.sum(jnp.where(lane == k, row[:, here - low:here - low + lanes], 0.0), axis=1, keepdims=True)
            scale = lax.rsqrt(pivot)
            pivot_row = row * scale
            column = jnp.sum(jnp.where(lane == k, work[top:, here:here + lanes], 0.0), axis=1, keepdims=True)
            column = jnp.where(row_id > k, column * scale, 0.0)
            work[top:, low:high] = work[top:, low:high] - column * pivot_row
            work[pl.ds(k, 1), low:high] = pivot_row
            return carry

        lax.fori_loop(0, tile, step, 0)


def inverse_kernel(a_ref, o_ref, work):
    size = a_ref.shape[0]
    half = size // 2
    rows_i = lax.broadcasted_iota(jnp.int32, (size, size), 0)
    cols_i = lax.broadcasted_iota(jnp.int32, (size, size), 1)
    diagonal = rows_i == cols_i
    a = a_ref[...]
    level = jnp.sum(jnp.where(diagonal, a, 0.0)) / size
    a = a + jnp.where(diagonal, 0.1 * level, 0.0)
    eye = jnp.where(diagonal[:half, :half], 1.0, 0.0).astype(a.dtype)
    hi = lax.Precision.HIGHEST
    nt = (((1,), (1,)), ((), ()))

    work[:, :half] = a[:half, :half]
    work[:, half:] = eye
    eliminate(work, half)
    inv11 = work[:, half:]
    low21 = lax.dot_general(a[half:, :half], inv11, nt, precision=hi, preferred_element_type=jnp.float32)
    schur = a[half:, half:] - lax.dot_general(low21, low21, nt, precision=hi, preferred_element_type=jnp.float32)
    work[:, :half] = schur
    work[:, half:] = eye
    eliminate(work, half)
    inv22 = work[:, half:]
    mid = jnp.dot(inv22, low21, precision=hi, preferred_element_type=jnp.float32)
    inv21 = -jnp.dot(mid, inv11, precision=hi, preferred_element_type=jnp.float32)
    o_ref[:half, :half] = inv11
    o_ref[:half, half:] = jnp.zeros((half, half), a.dtype)
    o_ref[half:, :half] = inv21
    o_ref[half:, half:] = inv22


def lower_inverse(scaled):
    size = scaled.shape[0]
    return pl.pallas_call(
        inverse_kernel,
        out_shape=jax.ShapeDtypeStruct((size, size), scaled.dtype),
        in_specs=[pl.BlockSpec(memory_space=pltpu.VMEM)],
        out_specs=pl.BlockSpec(memory_space=pltpu.VMEM),
        scratch_shapes=[pltpu.VMEM((size // 2, size), scaled.dtype)],
    )(scaled)


def whitener(scaled):
    return lower_inverse(scaled).T


def mm(left, right):
    return jnp.dot(left, right, precision=lax.Precision.HIGHEST)


def tmm(left, right):
    return gram_of(left, right)


def per_device(snapshots):
    local_rows = snapshots.shape[0]
    total = local_rows * lax.axis_size("rows")
    width = snapshots.shape[1] // 2
    count = lax.axis_size("pairs")
    index = lax.axis_index("pairs")
    first = index == 0
    last = index == count - 1
    pair = snapshots

    gram = allreduce_rows(gram_of(pair, pair)) / total
    sent, gram = lax.optimization_barrier((pair, gram))
    left = from_behind(sent[:, :width], "pairs", 1)
    right = lax.ppermute(sent[:, width:], "pairs", [(0, 1)])
    raw_a = jnp.where(first, pair, jnp.concatenate([left, right], axis=1))
    raw_b = jnp.where(last, pair, from_behind(sent, "pairs", -1))


    whiten = whitener(gram)
    moment = tmm(whiten, mm(gram, whiten))
    top = jnp.concatenate([whiten[:, :width], moment[:width, :width]], axis=0)
    bottom = jnp.concatenate([whiten[:, width:], moment[width:, width:]], axis=0)
    outgoing = jnp.where(first, bottom, top)
    arrived_a = from_behind(outgoing, "pairs", 1)
    arrived_b = from_behind(bottom, "pairs", -1)
    side_a = jnp.where(first, top, arrived_a)
    side_b = jnp.where(last, top, arrived_b)
    rows = whiten.shape[0]
    x_a, m_a = side_a[:rows], side_a[rows:]
    x_b, m_b = side_b[:rows], side_b[rows:]

    off = allreduce_rows(tmm(x_a, mm(gram_of(raw_a, raw_b), x_b)), 1) / total
    gram2 = jnp.concatenate(
        [jnp.concatenate([m_a, off], axis=1), jnp.concatenate([off.T, m_b], axis=1)], axis=0
    )
    whiten2 = whitener(gram2)
    combined = jnp.concatenate([mm(x_a, whiten2[:width]), mm(x_b, whiten2[width:])], axis=0)
    return mm(jnp.concatenate([raw_a, raw_b], axis=1), combined)


def solution(mesh):
    return jax.shard_map(
        per_device,
        mesh=mesh,
        in_specs=(P("rows", "pairs"),),
        out_specs=P("rows", "pairs"),
        check_vma=False,
    )
```

```python
import functools

import jax
import jax.numpy as jnp
from jax import lax
from jax.experimental import pallas as pl
from jax.experimental.pallas import tpu as pltpu
from jax.sharding import PartitionSpec as P

MESH = pl.DeviceIdType.MESH


def from_behind(value, axis, steps):
    count = lax.axis_size(axis)
    leading, last = (max(0, -steps), min(count, count - steps))
    return lax.ppermute(value, axis, [(source, source + steps) for source in range(leading, last)])


def gram_of(left, right):
    return lax.dot_general(left, right, (((0,), (0,)), ((), ())), precision=lax.Precision.HIGHEST)


def allreduce_kernel(n, chunk, g_ref, o_ref, recv, send_sem, recv_sem, send2_sem, recv2_sem):
    me = lax.axis_index("rows")
    col = lax.axis_index("pairs")

    barrier = pltpu.get_barrier_semaphore()
    for d in range(1, n):
        peer = lax.rem(me + d, n)
        pl.semaphore_signal(barrier, inc=1, device_id=(peer, col), device_id_type=MESH)
    pl.semaphore_wait(barrier, n - 1)

    scatter = []
    for d in range(1, n):
        peer = lax.rem(me + d, n)
        start = pl.multiple_of(peer * chunk, chunk)
        copy = pltpu.make_async_remote_copy(
            src_ref=g_ref.at[pl.ds(start, chunk), :],
            dst_ref=recv.at[d],
            send_sem=send_sem.at[d],
            recv_sem=recv_sem.at[d],
            device_id=(peer, col),
            device_id_type=MESH,
        )
        copy.start()
        scatter.append(copy)

    mine = pl.multiple_of(me * chunk, chunk)
    total = g_ref[pl.ds(mine, chunk), :]
    for d in range(1, n):
        scatter[d - 1].wait_recv()
        total = total + recv[d]
    o_ref[pl.ds(mine, chunk), :] = total
    for copy in scatter:
        copy.wait_send()

    gather = []
    for d in range(1, n):
        peer = lax.rem(me + d, n)
        copy = pltpu.make_async_remote_copy(
            src_ref=o_ref.at[pl.ds(mine, chunk), :],
            dst_ref=o_ref.at[pl.ds(mine, chunk), :],
            send_sem=send2_sem.at[d],
            recv_sem=recv2_sem.at[d],
            device_id=(peer, col),
            device_id_type=MESH,
        )
        copy.start()
        gather.append(copy)
    for d in range(1, n):
        source = lax.rem(me + n - d, n)
        start = pl.multiple_of(source * chunk, chunk)
        pltpu.make_async_remote_copy(
            src_ref=o_ref.at[pl.ds(start, chunk), :],
            dst_ref=o_ref.at[pl.ds(start, chunk), :],
            send_sem=send2_sem.at[d],
            recv_sem=recv2_sem.at[d],
            device_id=(source, col),
            device_id_type=MESH,
        ).wait_recv()
    for copy in gather:
        copy.wait_send()


def allreduce_rows(g, key=0):
    n = lax.axis_size("rows")
    rows, cols = g.shape
    chunk = rows // n
    return pl.pallas_call(
        functools.partial(allreduce_kernel, n, chunk),
        out_shape=jax.ShapeDtypeStruct((rows, cols), g.dtype),
        in_specs=[pl.BlockSpec(memory_space=pltpu.VMEM)],
        out_specs=pl.BlockSpec(memory_space=pltpu.VMEM),
        scratch_shapes=[
            pltpu.VMEM((n, chunk, cols), g.dtype),
            pltpu.SemaphoreType.DMA((n,)),
            pltpu.SemaphoreType.DMA((n,)),
            pltpu.SemaphoreType.DMA((n,)),
            pltpu.SemaphoreType.DMA((n,)),
        ],
        compiler_params=pltpu.CompilerParams(collective_id=key, has_side_effects=True),
    )(g)


def eliminate(work, size):
    tile = 8
    lanes = 128
    for block in range(size // tile):
        top = block * tile
        low = (top // lanes) * lanes
        high = size + min(size, ((top + tile + lanes - 1) // lanes) * lanes)
        height = size - top
        here = (top // lanes) * lanes
        lane = lax.broadcasted_iota(jnp.int32, (1, lanes), 1) + here
        row_id = lax.broadcasted_iota(jnp.int32, (height, 1), 0) + top

        def step(t, carry, top=top, low=low, high=high, here=here, lane=lane, row_id=row_id):
            k = top + t
            row = work[pl.ds(k, 1), low:high]
            pivot = jnp.sum(jnp.where(lane == k, row[:, here - low:here - low + lanes], 0.0), axis=1, keepdims=True)
            scale = lax.rsqrt(pivot)
            pivot_row = row * scale
            column = jnp.sum(jnp.where(lane == k, work[top:, here:here + lanes], 0.0), axis=1, keepdims=True)
            column = jnp.where(row_id > k, column * scale, 0.0)
            work[top:, low:high] = work[top:, low:high] - column * pivot_row
            work[pl.ds(k, 1), low:high] = pivot_row
            return carry

        lax.fori_loop(0, tile, step, 0, unroll=True)


def inverse_kernel(a_ref, o_ref, work):
    size = a_ref.shape[0]
    half = size // 2
    rows_i = lax.broadcasted_iota(jnp.int32, (size, size), 0)
    cols_i = lax.broadcasted_iota(jnp.int32, (size, size), 1)
    diagonal = rows_i == cols_i
    a = a_ref[...]
    level = jnp.sum(jnp.where(diagonal, a, 0.0)) / size
    a = a + jnp.where(diagonal, 0.1 * level, 0.0)
    eye = jnp.where(diagonal[:half, :half], 1.0, 0.0).astype(a.dtype)
    hi = lax.Precision.HIGHEST
    nt = (((1,), (1,)), ((), ()))

    work[:, :half] = a[:half, :half]
    work[:, half:] = eye
    eliminate(work, half)
    inv11 = work[:, half:]
    low21 = lax.dot_general(a[half:, :half], inv11, nt, precision=hi, preferred_element_type=jnp.float32)
    schur = a[half:, half:] - lax.dot_general(low21, low21, nt, precision=hi, preferred_element_type=jnp.float32)
    work[:, :half] = schur
    work[:, half:] = eye
    eliminate(work, half)
    inv22 = work[:, half:]
    mid = jnp.dot(inv22, low21, precision=hi, preferred_element_type=jnp.float32)
    inv21 = -jnp.dot(mid, inv11, precision=hi, preferred_element_type=jnp.float32)
    o_ref[:half, :half] = inv11
    o_ref[:half, half:] = jnp.zeros((half, half), a.dtype)
    o_ref[half:, :half] = inv21
    o_ref[half:, half:] = inv22


def lower_inverse(scaled):
    size = scaled.shape[0]
    return pl.pallas_call(
        inverse_kernel,
        out_shape=jax.ShapeDtypeStruct((size, size), scaled.dtype),
        in_specs=[pl.BlockSpec(memory_space=pltpu.VMEM)],
        out_specs=pl.BlockSpec(memory_space=pltpu.VMEM),
        scratch_shapes=[pltpu.VMEM((size // 2, size), scaled.dtype)],
    )(scaled)


def whitener(scaled):
    return lower_inverse(scaled).T


def mm(left, right):
    return jnp.dot(left, right, precision=lax.Precision.HIGHEST)


def tmm(left, right):
    return gram_of(left, right)


def per_device(snapshots):
    local_rows = snapshots.shape[0]
    total = local_rows * lax.axis_size("rows")
    width = snapshots.shape[1] // 2
    count = lax.axis_size("pairs")
    index = lax.axis_index("pairs")
    first = index == 0
    last = index == count - 1
    pair = snapshots

    gram = allreduce_rows(gram_of(pair, pair)) / total
    sent, gram = lax.optimization_barrier((pair, gram))
    left = from_behind(sent[:, :width], "pairs", 1)
    right = lax.ppermute(sent[:, width:], "pairs", [(0, 1)])
    raw_a = jnp.where(first, pair, jnp.concatenate([left, right], axis=1))
    raw_b = jnp.where(last, pair, from_behind(sent, "pairs", -1))


    whiten = whitener(gram)
    moment = tmm(whiten, mm(gram, whiten))
    top = jnp.concatenate([whiten[:, :width], moment[:width, :width]], axis=0)
    bottom = jnp.concatenate([whiten[:, width:], moment[width:, width:]], axis=0)
    outgoing = jnp.where(first, bottom, top)
    arrived_a = from_behind(outgoing, "pairs", 1)
    arrived_b = from_behind(bottom, "pairs", -1)
    side_a = jnp.where(first, top, arrived_a)
    side_b = jnp.where(last, top, arrived_b)
    rows = whiten.shape[0]
    x_a, m_a = side_a[:rows], side_a[rows:]
    x_b, m_b = side_b[:rows], side_b[rows:]

    off = allreduce_rows(tmm(x_a, mm(gram_of(raw_a, raw_b), x_b)), 1) / total
    gram2 = jnp.concatenate(
        [jnp.concatenate([m_a, off], axis=1), jnp.concatenate([off.T, m_b], axis=1)], axis=0
    )
    whiten2 = whitener(gram2)
    combined = jnp.concatenate([mm(x_a, whiten2[:width]), mm(x_b, whiten2[width:])], axis=0)
    return mm(jnp.concatenate([raw_a, raw_b], axis=1), combined)


def solution(mesh):
    return jax.shard_map(
        per_device,
        mesh=mesh,
        in_specs=(P("rows", "pairs"),),
        out_specs=P("rows", "pairs"),
        check_vma=False,
    )
```

```python
import functools

import jax
import jax.numpy as jnp
from jax import lax
from jax.experimental import pallas as pl
from jax.experimental.pallas import tpu as pltpu
from jax.sharding import PartitionSpec as P

MESH = pl.DeviceIdType.MESH


def from_behind(value, axis, steps):
    count = lax.axis_size(axis)
    leading, last = (max(0, -steps), min(count, count - steps))
    return lax.ppermute(value, axis, [(source, source + steps) for source in range(leading, last)])


def gram_of(left, right):
    return lax.dot_general(left, right, (((0,), (0,)), ((), ())), precision=lax.Precision.HIGHEST)


def allreduce_kernel(n, chunk, g_ref, o_ref, recv, send_sem, recv_sem, send2_sem, recv2_sem):
    me = lax.axis_index("rows")
    col = lax.axis_index("pairs")

    barrier = pltpu.get_barrier_semaphore()
    for d in range(1, n):
        peer = lax.rem(me + d, n)
        pl.semaphore_signal(barrier, inc=1, device_id=(peer, col), device_id_type=MESH)
    pl.semaphore_wait(barrier, n - 1)

    scatter = []
    for d in range(1, n):
        peer = lax.rem(me + d, n)
        start = pl.multiple_of(peer * chunk, chunk)
        copy = pltpu.make_async_remote_copy(
            src_ref=g_ref.at[pl.ds(start, chunk), :],
            dst_ref=recv.at[d],
            send_sem=send_sem.at[d],
            recv_sem=recv_sem.at[d],
            device_id=(peer, col),
            device_id_type=MESH,
        )
        copy.start()
        scatter.append(copy)

    mine = pl.multiple_of(me * chunk, chunk)
    total = g_ref[pl.ds(mine, chunk), :]
    for d in range(1, n):
        scatter[d - 1].wait_recv()
        total = total + recv[d]
    o_ref[pl.ds(mine, chunk), :] = total

    gather = []
    for d in range(1, n):
        peer = lax.rem(me + d, n)
        copy = pltpu.make_async_remote_copy(
            src_ref=o_ref.at[pl.ds(mine, chunk), :],
            dst_ref=o_ref.at[pl.ds(mine, chunk), :],
            send_sem=send2_sem.at[d],
            recv_sem=recv2_sem.at[d],
            device_id=(peer, col),
            device_id_type=MESH,
        )
        copy.start()
        gather.append(copy)
    for d in range(1, n):
        source = lax.rem(me + n - d, n)
        start = pl.multiple_of(source * chunk, chunk)
        pltpu.make_async_remote_copy(
            src_ref=o_ref.at[pl.ds(start, chunk), :],
            dst_ref=o_ref.at[pl.ds(start, chunk), :],
            send_sem=send2_sem.at[d],
            recv_sem=recv2_sem.at[d],
            device_id=(source, col),
            device_id_type=MESH,
        ).wait_recv()
    for copy in scatter + gather:
        copy.wait_send()


def allreduce_rows(g, key=0):
    n = lax.axis_size("rows")
    rows, cols = g.shape
    chunk = rows // n
    return pl.pallas_call(
        functools.partial(allreduce_kernel, n, chunk),
        out_shape=jax.ShapeDtypeStruct((rows, cols), g.dtype),
        in_specs=[pl.BlockSpec(memory_space=pltpu.VMEM)],
        out_specs=pl.BlockSpec(memory_space=pltpu.VMEM),
        scratch_shapes=[
            pltpu.VMEM((n, chunk, cols), g.dtype),
            pltpu.SemaphoreType.DMA((n,)),
            pltpu.SemaphoreType.DMA((n,)),
            pltpu.SemaphoreType.DMA((n,)),
            pltpu.SemaphoreType.DMA((n,)),
        ],
        compiler_params=pltpu.CompilerParams(collective_id=key, has_side_effects=True),
    )(g)


def eliminate(work, size):
    tile = 8
    lanes = 128
    for block in range(size // tile):
        top = block * tile
        low = (top // lanes) * lanes
        high = size + min(size, ((top + tile + lanes - 1) // lanes) * lanes)
        height = size - top
        here = (top // lanes) * lanes
        lane = lax.broadcasted_iota(jnp.int32, (1, lanes), 1) + here
        row_id = lax.broadcasted_iota(jnp.int32, (height, 1), 0) + top

        def step(t, carry, top=top, low=low, high=high, here=here, lane=lane, row_id=row_id):
            k = top + t
            row = work[pl.ds(k, 1), low:high]
            pivot = jnp.sum(jnp.where(lane == k, row[:, here - low:here - low + lanes], 0.0), axis=1, keepdims=True)
            scale = lax.rsqrt(pivot)
            pivot_row = row * scale
            column = jnp.sum(jnp.where(lane == k, work[top:, here:here + lanes], 0.0), axis=1, keepdims=True)
            column = jnp.where(row_id > k, column * scale, 0.0)
            work[top:, low:high] = work[top:, low:high] - column * pivot_row
            work[pl.ds(k, 1), low:high] = pivot_row
            return carry

        lax.fori_loop(0, tile, step, 0, unroll=True)


def inverse_kernel(a_ref, o_ref, work):
    size = a_ref.shape[0]
    half = size // 2
    rows_i = lax.broadcasted_iota(jnp.int32, (size, size), 0)
    cols_i = lax.broadcasted_iota(jnp.int32, (size, size), 1)
    diagonal = rows_i == cols_i
    a = a_ref[...]
    level = jnp.sum(jnp.where(diagonal, a, 0.0)) / size
    a = a + jnp.where(diagonal, 0.1 * level, 0.0)
    eye = jnp.where(diagonal[:half, :half], 1.0, 0.0).astype(a.dtype)
    hi = lax.Precision.HIGHEST
    nt = (((1,), (1,)), ((), ()))

    work[:, :half] = a[:half, :half]
    work[:, half:] = eye
    eliminate(work, half)
    inv11 = work[:, half:]
    low21 = lax.dot_general(a[half:, :half], inv11, nt, precision=hi, preferred_element_type=jnp.float32)
    schur = a[half:, half:] - lax.dot_general(low21, low21, nt, precision=hi, preferred_element_type=jnp.float32)
    work[:, :half] = schur
    work[:, half:] = eye
    eliminate(work, half)
    inv22 = work[:, half:]
    mid = jnp.dot(inv22, low21, precision=hi, preferred_element_type=jnp.float32)
    inv21 = -jnp.dot(mid, inv11, precision=hi, preferred_element_type=jnp.float32)
    o_ref[:half, :half] = inv11
    o_ref[:half, half:] = jnp.zeros((half, half), a.dtype)
    o_ref[half:, :half] = inv21
    o_ref[half:, half:] = inv22


def lower_inverse(scaled):
    size = scaled.shape[0]
    return pl.pallas_call(
        inverse_kernel,
        out_shape=jax.ShapeDtypeStruct((size, size), scaled.dtype),
        in_specs=[pl.BlockSpec(memory_space=pltpu.VMEM)],
        out_specs=pl.BlockSpec(memory_space=pltpu.VMEM),
        scratch_shapes=[pltpu.VMEM((size // 2, size), scaled.dtype)],
    )(scaled)


def whitener(scaled):
    return lower_inverse(scaled).T


def mm(left, right):
    return jnp.dot(left, right, precision=lax.Precision.HIGHEST)


def tmm(left, right):
    return gram_of(left, right)


def per_device(snapshots):
    local_rows = snapshots.shape[0]
    total = local_rows * lax.axis_size("rows")
    width = snapshots.shape[1] // 2
    count = lax.axis_size("pairs")
    index = lax.axis_index("pairs")
    first = index == 0
    last = index == count - 1
    pair = snapshots

    gram = allreduce_rows(gram_of(pair, pair)) / total
    sent, gram = lax.optimization_barrier((pair, gram))
    left = from_behind(sent[:, :width], "pairs", 1)
    right = lax.ppermute(sent[:, width:], "pairs", [(0, 1)])
    raw_a = jnp.where(first, pair, jnp.concatenate([left, right], axis=1))
    raw_b = jnp.where(last, pair, from_behind(sent, "pairs", -1))


    whiten = whitener(gram)
    moment = tmm(whiten, mm(gram, whiten))
    top = jnp.concatenate([whiten[:, :width], moment[:width, :width]], axis=0)
    bottom = jnp.concatenate([whiten[:, width:], moment[width:, width:]], axis=0)
    outgoing = jnp.where(first, bottom, top)
    arrived_a = from_behind(outgoing, "pairs", 1)
    arrived_b = from_behind(bottom, "pairs", -1)
    side_a = jnp.where(first, top, arrived_a)
    side_b = jnp.where(last, top, arrived_b)
    rows = whiten.shape[0]
    x_a, m_a = side_a[:rows], side_a[rows:]
    x_b, m_b = side_b[:rows], side_b[rows:]

    off = allreduce_rows(tmm(x_a, mm(gram_of(raw_a, raw_b), x_b)), 1) / total
    gram2 = jnp.concatenate(
        [jnp.concatenate([m_a, off], axis=1), jnp.concatenate([off.T, m_b], axis=1)], axis=0
    )
    whiten2 = whitener(gram2)
    combined = jnp.concatenate([mm(x_a, whiten2[:width]), mm(x_b, whiten2[width:])], axis=0)
    return mm(jnp.concatenate([raw_a, raw_b], axis=1), combined)


def solution(mesh):
    return jax.shard_map(
        per_device,
        mesh=mesh,
        in_specs=(P("rows", "pairs"),),
        out_specs=P("rows", "pairs"),
        check_vma=False,
    )
```

```python
import functools

import jax
import jax.numpy as jnp
from jax import lax
from jax.experimental import pallas as pl
from jax.experimental.pallas import tpu as pltpu
from jax.sharding import PartitionSpec as P

MESH = pl.DeviceIdType.MESH


def from_behind(value, axis, steps):
    count = lax.axis_size(axis)
    leading, last = (max(0, -steps), min(count, count - steps))
    return lax.ppermute(value, axis, [(source, source + steps) for source in range(leading, last)])


def gram_of(left, right):
    return lax.dot_general(left, right, (((0,), (0,)), ((), ())), precision=lax.Precision.HIGHEST)


def allreduce_kernel(n, chunk, g_ref, o_ref, recv, send_sem, recv_sem, send2_sem, recv2_sem):
    me = lax.axis_index("rows")
    col = lax.axis_index("pairs")

    barrier = pltpu.get_barrier_semaphore()
    for d in range(1, n):
        peer = lax.rem(me + d, n)
        pl.semaphore_signal(barrier, inc=1, device_id=(peer, col), device_id_type=MESH)
    pl.semaphore_wait(barrier, n - 1)

    scatter = []
    for d in range(1, n):
        peer = lax.rem(me + d, n)
        start = pl.multiple_of(peer * chunk, chunk)
        copy = pltpu.make_async_remote_copy(
            src_ref=g_ref.at[pl.ds(start, chunk), :],
            dst_ref=recv.at[d],
            send_sem=send_sem.at[d],
            recv_sem=recv_sem.at[d],
            device_id=(peer, col),
            device_id_type=MESH,
        )
        copy.start()
        scatter.append(copy)

    mine = pl.multiple_of(me * chunk, chunk)
    total = g_ref[pl.ds(mine, chunk), :]
    for d in range(1, n):
        scatter[d - 1].wait_recv()
        total = total + recv[d]
    o_ref[pl.ds(mine, chunk), :] = total

    gather = []
    for d in range(1, n):
        peer = lax.rem(me + d, n)
        copy = pltpu.make_async_remote_copy(
            src_ref=o_ref.at[pl.ds(mine, chunk), :],
            dst_ref=o_ref.at[pl.ds(mine, chunk), :],
            send_sem=send2_sem.at[d],
            recv_sem=recv2_sem.at[d],
            device_id=(peer, col),
            device_id_type=MESH,
        )
        copy.start()
        gather.append(copy)
    for d in range(1, n):
        source = lax.rem(me + n - d, n)
        start = pl.multiple_of(source * chunk, chunk)
        pltpu.make_async_remote_copy(
            src_ref=o_ref.at[pl.ds(start, chunk), :],
            dst_ref=o_ref.at[pl.ds(start, chunk), :],
            send_sem=send2_sem.at[d],
            recv_sem=recv2_sem.at[d],
            device_id=(source, col),
            device_id_type=MESH,
        ).wait_recv()
    for copy in scatter + gather:
        copy.wait_send()


def allreduce_rows(g, key=0):
    n = lax.axis_size("rows")
    rows, cols = g.shape
    chunk = rows // n
    return pl.pallas_call(
        functools.partial(allreduce_kernel, n, chunk),
        out_shape=jax.ShapeDtypeStruct((rows, cols), g.dtype),
        in_specs=[pl.BlockSpec(memory_space=pltpu.VMEM)],
        out_specs=pl.BlockSpec(memory_space=pltpu.VMEM),
        scratch_shapes=[
            pltpu.VMEM((n, chunk, cols), g.dtype),
            pltpu.SemaphoreType.DMA((n,)),
            pltpu.SemaphoreType.DMA((n,)),
            pltpu.SemaphoreType.DMA((n,)),
            pltpu.SemaphoreType.DMA((n,)),
        ],
        compiler_params=pltpu.CompilerParams(collective_id=key, has_side_effects=True),
    )(g)


def eliminate(work, size):
    tile = 8
    lanes = 128
    for block in range(size // tile):
        top = block * tile
        low = (top // lanes) * lanes
        high = size + min(size, ((top + tile + lanes - 1) // lanes) * lanes)
        height = size - top
        here = (top // lanes) * lanes
        lane = lax.broadcasted_iota(jnp.int32, (1, lanes), 1) + here
        row_id = lax.broadcasted_iota(jnp.int32, (height, 1), 0) + top

        def step(t, carry, top=top, low=low, high=high, here=here, lane=lane, row_id=row_id):
            k = top + t
            row = work[pl.ds(k, 1), low:high]
            pivot = jnp.sum(jnp.where(lane == k, row[:, here - low:here - low + lanes], 0.0), axis=1, keepdims=True)
            scale = lax.rsqrt(pivot)
            pivot_row = row * scale
            part = work[top:, low:high]
            column = jnp.sum(jnp.where(lane == k, part[:, here - low:here - low + lanes], 0.0), axis=1, keepdims=True)
            column = jnp.where(row_id > k, column * scale, 0.0)
            work[top:, low:high] = part - column * pivot_row
            work[pl.ds(k, 1), low:high] = pivot_row
            return carry

        lax.fori_loop(0, tile, step, 0, unroll=True)


def inverse_kernel(a_ref, o_ref, work):
    size = a_ref.shape[0]
    half = size // 2
    rows_i = lax.broadcasted_iota(jnp.int32, (size, size), 0)
    cols_i = lax.broadcasted_iota(jnp.int32, (size, size), 1)
    diagonal = rows_i == cols_i
    a = a_ref[...]
    level = jnp.sum(jnp.where(diagonal, a, 0.0)) / size
    a = a + jnp.where(diagonal, 0.1 * level, 0.0)
    eye = jnp.where(diagonal[:half, :half], 1.0, 0.0).astype(a.dtype)
    hi = lax.Precision.HIGHEST
    nt = (((1,), (1,)), ((), ()))

    work[:, :half] = a[:half, :half]
    work[:, half:] = eye
    eliminate(work, half)
    inv11 = work[:, half:]
    low21 = lax.dot_general(a[half:, :half], inv11, nt, precision=hi, preferred_element_type=jnp.float32)
    schur = a[half:, half:] - lax.dot_general(low21, low21, nt, precision=hi, preferred_element_type=jnp.float32)
    work[:, :half] = schur
    work[:, half:] = eye
    eliminate(work, half)
    inv22 = work[:, half:]
    mid = jnp.dot(inv22, low21, precision=hi, preferred_element_type=jnp.float32)
    inv21 = -jnp.dot(mid, inv11, precision=hi, preferred_element_type=jnp.float32)
    o_ref[:half, :half] = inv11
    o_ref[:half, half:] = jnp.zeros((half, half), a.dtype)
    o_ref[half:, :half] = inv21
    o_ref[half:, half:] = inv22


def lower_inverse(scaled):
    size = scaled.shape[0]
    return pl.pallas_call(
        inverse_kernel,
        out_shape=jax.ShapeDtypeStruct((size, size), scaled.dtype),
        in_specs=[pl.BlockSpec(memory_space=pltpu.VMEM)],
        out_specs=pl.BlockSpec(memory_space=pltpu.VMEM),
        scratch_shapes=[pltpu.VMEM((size // 2, size), scaled.dtype)],
    )(scaled)


def whitener(scaled):
    return lower_inverse(scaled).T


def mm(left, right):
    return jnp.dot(left, right, precision=lax.Precision.HIGHEST)


def tmm(left, right):
    return gram_of(left, right)


def per_device(snapshots):
    local_rows = snapshots.shape[0]
    total = local_rows * lax.axis_size("rows")
    width = snapshots.shape[1] // 2
    count = lax.axis_size("pairs")
    index = lax.axis_index("pairs")
    first = index == 0
    last = index == count - 1
    pair = snapshots

    gram = allreduce_rows(gram_of(pair, pair)) / total
    sent, gram = lax.optimization_barrier((pair, gram))
    left = from_behind(sent[:, :width], "pairs", 1)
    right = lax.ppermute(sent[:, width:], "pairs", [(0, 1)])
    raw_a = jnp.where(first, pair, jnp.concatenate([left, right], axis=1))
    raw_b = jnp.where(last, pair, from_behind(sent, "pairs", -1))


    whiten = whitener(gram)
    moment = tmm(whiten, mm(gram, whiten))
    top = jnp.concatenate([whiten[:, :width], moment[:width, :width]], axis=0)
    bottom = jnp.concatenate([whiten[:, width:], moment[width:, width:]], axis=0)
    outgoing = jnp.where(first, bottom, top)
    arrived_a = from_behind(outgoing, "pairs", 1)
    arrived_b = from_behind(bottom, "pairs", -1)
    side_a = jnp.where(first, top, arrived_a)
    side_b = jnp.where(last, top, arrived_b)
    rows = whiten.shape[0]
    x_a, m_a = side_a[:rows], side_a[rows:]
    x_b, m_b = side_b[:rows], side_b[rows:]

    off = allreduce_rows(tmm(x_a, mm(gram_of(raw_a, raw_b), x_b)), 1) / total
    gram2 = jnp.concatenate(
        [jnp.concatenate([m_a, off], axis=1), jnp.concatenate([off.T, m_b], axis=1)], axis=0
    )
    whiten2 = whitener(gram2)
    combined = jnp.concatenate([mm(x_a, whiten2[:width]), mm(x_b, whiten2[width:])], axis=0)
    return mm(jnp.concatenate([raw_a, raw_b], axis=1), combined)


def solution(mesh):
    return jax.shard_map(
        per_device,
        mesh=mesh,
        in_specs=(P("rows", "pairs"),),
        out_specs=P("rows", "pairs"),
        check_vma=False,
    )
```

```python
import functools

import jax
import jax.numpy as jnp
from jax import lax
from jax.experimental import pallas as pl
from jax.experimental.pallas import tpu as pltpu
from jax.sharding import PartitionSpec as P

MESH = pl.DeviceIdType.MESH


def from_behind(value, axis, steps):
    count = lax.axis_size(axis)
    leading, last = (max(0, -steps), min(count, count - steps))
    return lax.ppermute(value, axis, [(source, source + steps) for source in range(leading, last)])


def gram_of(left, right):
    return lax.dot_general(left, right, (((0,), (0,)), ((), ())), precision=lax.Precision.HIGHEST)


def allreduce_kernel(n, chunk, g_ref, o_ref, recv, send_sem, recv_sem, send2_sem, recv2_sem):
    me = lax.axis_index("rows")
    col = lax.axis_index("pairs")

    barrier = pltpu.get_barrier_semaphore()
    for d in range(1, n):
        peer = lax.rem(me + d, n)
        pl.semaphore_signal(barrier, inc=1, device_id=(peer, col), device_id_type=MESH)
    pl.semaphore_wait(barrier, n - 1)

    scatter = []
    for d in range(1, n):
        peer = lax.rem(me + d, n)
        start = pl.multiple_of(peer * chunk, chunk)
        copy = pltpu.make_async_remote_copy(
            src_ref=g_ref.at[pl.ds(start, chunk), :],
            dst_ref=recv.at[d],
            send_sem=send_sem.at[d],
            recv_sem=recv_sem.at[d],
            device_id=(peer, col),
            device_id_type=MESH,
        )
        copy.start()
        scatter.append(copy)

    mine = pl.multiple_of(me * chunk, chunk)
    total = g_ref[pl.ds(mine, chunk), :]
    for d in range(1, n):
        scatter[d - 1].wait_recv()
        total = total + recv[d]
    o_ref[pl.ds(mine, chunk), :] = total

    gather = []
    for d in range(1, n):
        peer = lax.rem(me + d, n)
        copy = pltpu.make_async_remote_copy(
            src_ref=o_ref.at[pl.ds(mine, chunk), :],
            dst_ref=o_ref.at[pl.ds(mine, chunk), :],
            send_sem=send2_sem.at[d],
            recv_sem=recv2_sem.at[d],
            device_id=(peer, col),
            device_id_type=MESH,
        )
        copy.start()
        gather.append(copy)
    for d in range(1, n):
        source = lax.rem(me + n - d, n)
        start = pl.multiple_of(source * chunk, chunk)
        pltpu.make_async_remote_copy(
            src_ref=o_ref.at[pl.ds(start, chunk), :],
            dst_ref=o_ref.at[pl.ds(start, chunk), :],
            send_sem=send2_sem.at[d],
            recv_sem=recv2_sem.at[d],
            device_id=(source, col),
            device_id_type=MESH,
        ).wait_recv()
    for copy in scatter + gather:
        copy.wait_send()


def allreduce_rows(g, key=0):
    n = lax.axis_size("rows")
    rows, cols = g.shape
    chunk = rows // n
    return pl.pallas_call(
        functools.partial(allreduce_kernel, n, chunk),
        out_shape=jax.ShapeDtypeStruct((rows, cols), g.dtype),
        in_specs=[pl.BlockSpec(memory_space=pltpu.VMEM)],
        out_specs=pl.BlockSpec(memory_space=pltpu.VMEM),
        scratch_shapes=[
            pltpu.VMEM((n, chunk, cols), g.dtype),
            pltpu.SemaphoreType.DMA((n,)),
            pltpu.SemaphoreType.DMA((n,)),
            pltpu.SemaphoreType.DMA((n,)),
            pltpu.SemaphoreType.DMA((n,)),
        ],
        compiler_params=pltpu.CompilerParams(collective_id=key, has_side_effects=True),
    )(g)


def eliminate(work, size):
    tile = 8
    lanes = 128
    for block in range(size // tile):
        top = block * tile
        low = (top // lanes) * lanes
        high = size + min(size, ((top + tile + lanes - 1) // lanes) * lanes)
        height = size - top
        here = (top // lanes) * lanes
        lane = lax.broadcasted_iota(jnp.int32, (1, lanes), 1) + here
        row_id = lax.broadcasted_iota(jnp.int32, (height, 1), 0) + top

        def step(t, carry, top=top, low=low, high=high, here=here, lane=lane, row_id=row_id):
            k = top + t
            row = work[pl.ds(k, 1), low:high]
            pivot = jnp.sum(jnp.where(lane == k, row[:, here - low:here - low + lanes], 0.0), axis=1, keepdims=True)
            scale = lax.rsqrt(pivot)
            pivot_row = row * scale
            column = jnp.sum(jnp.where(lane == k, work[top:, here:here + lanes], 0.0), axis=1, keepdims=True)
            column = jnp.where(row_id > k, column * scale, 0.0)
            work[top:, low:high] = work[top:, low:high] - column * pivot_row
            work[pl.ds(k, 1), low:high] = pivot_row
            return carry

        lax.fori_loop(0, tile, step, 0, unroll=True)


def inverse_kernel(a_ref, o_ref, work):
    size = a_ref.shape[0]
    half = size // 2
    rows_i = lax.broadcasted_iota(jnp.int32, (size, size), 0)
    cols_i = lax.broadcasted_iota(jnp.int32, (size, size), 1)
    diagonal = rows_i == cols_i
    a = a_ref[...]
    level = jnp.sum(jnp.where(diagonal, a, 0.0)) / size
    a = a + jnp.where(diagonal, 0.1 * level, 0.0)
    eye = jnp.where(diagonal[:half, :half], 1.0, 0.0).astype(a.dtype)
    hi = lax.Precision.HIGHEST
    nt = (((1,), (1,)), ((), ()))

    work[:, :half] = a[:half, :half]
    work[:, half:] = eye
    eliminate(work, half)
    inv11 = work[:, half:]
    low21 = lax.dot_general(a[half:, :half], inv11, nt, precision=hi, preferred_element_type=jnp.float32)
    schur = a[half:, half:] - lax.dot_general(low21, low21, nt, precision=hi, preferred_element_type=jnp.float32)
    work[:, :half] = schur
    work[:, half:] = eye
    eliminate(work, half)
    inv22 = work[:, half:]
    mid = jnp.dot(inv22, low21, precision=hi, preferred_element_type=jnp.float32)
    inv21 = -jnp.dot(mid, inv11, precision=hi, preferred_element_type=jnp.float32)
    o_ref[:half, :half] = inv11
    o_ref[:half, half:] = jnp.zeros((half, half), a.dtype)
    o_ref[half:, :half] = inv21
    o_ref[half:, half:] = inv22


def lower_inverse(scaled):
    size = scaled.shape[0]
    return pl.pallas_call(
        inverse_kernel,
        out_shape=jax.ShapeDtypeStruct((size, size), scaled.dtype),
        in_specs=[pl.BlockSpec(memory_space=pltpu.VMEM)],
        out_specs=pl.BlockSpec(memory_space=pltpu.VMEM),
        scratch_shapes=[pltpu.VMEM((size // 2, size), scaled.dtype)],
    )(scaled)


def whitener(scaled):
    return lower_inverse(scaled).T


def mm(left, right):
    return jnp.dot(left, right, precision=lax.Precision.HIGHEST)


def tmm(left, right):
    return gram_of(left, right)


def per_device(snapshots):
    local_rows = snapshots.shape[0]
    total = local_rows * lax.axis_size("rows")
    width = snapshots.shape[1] // 2
    count = lax.axis_size("pairs")
    index = lax.axis_index("pairs")
    first = index == 0
    last = index == count - 1
    pair = snapshots

    lead, rest = pair[:, :width], pair[:, width:]
    below = gram_of(rest, lead)
    local = jnp.concatenate(
        [jnp.concatenate([gram_of(lead, lead), below.T], axis=1), jnp.concatenate([below, gram_of(rest, rest)], axis=1)],
        axis=0,
    )
    gram = allreduce_rows(local) / total
    sent, gram = lax.optimization_barrier((pair, gram))
    left = from_behind(sent[:, :width], "pairs", 1)
    right = lax.ppermute(sent[:, width:], "pairs", [(0, 1)])
    raw_a = jnp.where(first, pair, jnp.concatenate([left, right], axis=1))
    raw_b = jnp.where(last, pair, from_behind(sent, "pairs", -1))


    whiten = whitener(gram)
    moment = tmm(whiten, mm(gram, whiten))
    top = jnp.concatenate([whiten[:, :width], moment[:width, :width]], axis=0)
    bottom = jnp.concatenate([whiten[:, width:], moment[width:, width:]], axis=0)
    outgoing = jnp.where(first, bottom, top)
    arrived_a = from_behind(outgoing, "pairs", 1)
    arrived_b = from_behind(bottom, "pairs", -1)
    side_a = jnp.where(first, top, arrived_a)
    side_b = jnp.where(last, top, arrived_b)
    rows = whiten.shape[0]
    x_a, m_a = side_a[:rows], side_a[rows:]
    x_b, m_b = side_b[:rows], side_b[rows:]

    off = allreduce_rows(tmm(x_a, mm(gram_of(raw_a, raw_b), x_b)), 1) / total
    gram2 = jnp.concatenate(
        [jnp.concatenate([m_a, off], axis=1), jnp.concatenate([off.T, m_b], axis=1)], axis=0
    )
    whiten2 = whitener(gram2)
    combined = jnp.concatenate([mm(x_a, whiten2[:width]), mm(x_b, whiten2[width:])], axis=0)
    return mm(jnp.concatenate([raw_a, raw_b], axis=1), combined)


def solution(mesh):
    return jax.shard_map(
        per_device,
        mesh=mesh,
        in_specs=(P("rows", "pairs"),),
        out_specs=P("rows", "pairs"),
        check_vma=False,
    )
```

```python
import functools

import jax
import jax.numpy as jnp
from jax import lax
from jax.experimental import pallas as pl
from jax.experimental.pallas import tpu as pltpu
from jax.sharding import PartitionSpec as P

MESH = pl.DeviceIdType.MESH


def from_behind(value, axis, steps):
    count = lax.axis_size(axis)
    leading, last = (max(0, -steps), min(count, count - steps))
    return lax.ppermute(value, axis, [(source, source + steps) for source in range(leading, last)])


def gram_of(left, right):
    return lax.dot_general(left, right, (((0,), (0,)), ((), ())), precision=lax.Precision.HIGHEST)


def allreduce_kernel(n, chunk, g_ref, o_ref, recv, send_sem, recv_sem, send2_sem, recv2_sem):
    me = lax.axis_index("rows")
    col = lax.axis_index("pairs")

    barrier = pltpu.get_barrier_semaphore()
    for d in range(1, n):
        peer = lax.rem(me + d, n)
        pl.semaphore_signal(barrier, inc=1, device_id=(peer, col), device_id_type=MESH)
    pl.semaphore_wait(barrier, n - 1)

    scatter = []
    for d in range(1, n):
        peer = lax.rem(me + d, n)
        start = pl.multiple_of(peer * chunk, chunk)
        copy = pltpu.make_async_remote_copy(
            src_ref=g_ref.at[pl.ds(start, chunk), :],
            dst_ref=recv.at[d],
            send_sem=send_sem.at[d],
            recv_sem=recv_sem.at[d],
            device_id=(peer, col),
            device_id_type=MESH,
        )
        copy.start()
        scatter.append(copy)

    mine = pl.multiple_of(me * chunk, chunk)
    total = g_ref[pl.ds(mine, chunk), :]
    for d in range(1, n):
        scatter[d - 1].wait_recv()
        total = total + recv[d]
    o_ref[pl.ds(mine, chunk), :] = total

    gather = []
    for d in range(1, n):
        peer = lax.rem(me + d, n)
        copy = pltpu.make_async_remote_copy(
            src_ref=o_ref.at[pl.ds(mine, chunk), :],
            dst_ref=o_ref.at[pl.ds(mine, chunk), :],
            send_sem=send2_sem.at[d],
            recv_sem=recv2_sem.at[d],
            device_id=(peer, col),
            device_id_type=MESH,
        )
        copy.start()
        gather.append(copy)
    for d in range(1, n):
        source = lax.rem(me + n - d, n)
        start = pl.multiple_of(source * chunk, chunk)
        pltpu.make_async_remote_copy(
            src_ref=o_ref.at[pl.ds(start, chunk), :],
            dst_ref=o_ref.at[pl.ds(start, chunk), :],
            send_sem=send2_sem.at[d],
            recv_sem=recv2_sem.at[d],
            device_id=(source, col),
            device_id_type=MESH,
        ).wait_recv()
    for copy in scatter + gather:
        copy.wait_send()


def allreduce_rows(g, key=0):
    n = lax.axis_size("rows")
    rows, cols = g.shape
    chunk = rows // n
    return pl.pallas_call(
        functools.partial(allreduce_kernel, n, chunk),
        out_shape=jax.ShapeDtypeStruct((rows, cols), g.dtype),
        in_specs=[pl.BlockSpec(memory_space=pltpu.VMEM)],
        out_specs=pl.BlockSpec(memory_space=pltpu.VMEM),
        scratch_shapes=[
            pltpu.VMEM((n, chunk, cols), g.dtype),
            pltpu.SemaphoreType.DMA((n,)),
            pltpu.SemaphoreType.DMA((n,)),
            pltpu.SemaphoreType.DMA((n,)),
            pltpu.SemaphoreType.DMA((n,)),
        ],
        compiler_params=pltpu.CompilerParams(collective_id=key, has_side_effects=True),
    )(g)


def eliminate(work, size):
    tile = 8
    lanes = 128
    for block in range(size // tile):
        top = block * tile
        low = (top // lanes) * lanes
        high = size + min(size, ((top + tile + lanes - 1) // lanes) * lanes)
        height = size - top
        here = (top // lanes) * lanes
        lane = lax.broadcasted_iota(jnp.int32, (1, lanes), 1) + here
        row_id = lax.broadcasted_iota(jnp.int32, (height, 1), 0) + top

        def step(t, carry, top=top, low=low, high=high, here=here, lane=lane, row_id=row_id):
            k = top + t
            row = work[pl.ds(k, 1), low:high]
            pivot = jnp.sum(jnp.where(lane == k, row[:, here - low:here - low + lanes], 0.0), axis=1, keepdims=True)
            scale = lax.rsqrt(pivot)
            pivot_row = row * scale
            column = jnp.sum(jnp.where(lane == k, work[top:, here:here + lanes], 0.0), axis=1, keepdims=True)
            column = jnp.where(row_id > k, column * scale, 0.0)
            work[top:, low:high] = work[top:, low:high] - column * pivot_row
            work[pl.ds(k, 1), low:high] = pivot_row
            return carry

        lax.fori_loop(0, tile, step, 0, unroll=True)


def inverse_kernel(a_ref, o_ref, work):
    size = a_ref.shape[0]
    half = size // 2
    rows_i = lax.broadcasted_iota(jnp.int32, (size, size), 0)
    cols_i = lax.broadcasted_iota(jnp.int32, (size, size), 1)
    diagonal = rows_i == cols_i
    a = a_ref[...]
    level = jnp.sum(jnp.where(diagonal, a, 0.0)) / size
    a = a + jnp.where(diagonal, 0.1 * level, 0.0)
    eye = jnp.where(diagonal[:half, :half], 1.0, 0.0).astype(a.dtype)
    hi = lax.Precision.HIGHEST
    nt = (((1,), (1,)), ((), ()))

    work[:, :half] = a[:half, :half]
    work[:, half:] = eye
    eliminate(work, half)
    inv11 = work[:, half:]
    low21 = lax.dot_general(a[half:, :half], inv11, nt, precision=hi, preferred_element_type=jnp.float32)
    schur = a[half:, half:] - lax.dot_general(low21, low21, nt, precision=hi, preferred_element_type=jnp.float32)
    work[:, :half] = schur
    work[:, half:] = eye
    eliminate(work, half)
    inv22 = work[:, half:]
    mid = jnp.dot(inv22, low21, precision=hi, preferred_element_type=jnp.float32)
    inv21 = -jnp.dot(mid, inv11, precision=hi, preferred_element_type=jnp.float32)
    o_ref[:half, :half] = inv11
    o_ref[:half, half:] = jnp.zeros((half, half), a.dtype)
    o_ref[half:, :half] = inv21
    o_ref[half:, half:] = inv22


def lower_inverse(scaled):
    size = scaled.shape[0]
    return pl.pallas_call(
        inverse_kernel,
        out_shape=jax.ShapeDtypeStruct((size, size), scaled.dtype),
        in_specs=[pl.BlockSpec(memory_space=pltpu.VMEM)],
        out_specs=pl.BlockSpec(memory_space=pltpu.VMEM),
        scratch_shapes=[pltpu.VMEM((size // 2, size), scaled.dtype)],
    )(scaled)


def whitener(scaled):
    return lower_inverse(scaled).T


def mm(left, right):
    return jnp.dot(left, right, precision=lax.Precision.HIGHEST)


def tmm(left, right):
    return gram_of(left, right)


def per_device(snapshots):
    local_rows = snapshots.shape[0]
    total = local_rows * lax.axis_size("rows")
    width = snapshots.shape[1] // 2
    count = lax.axis_size("pairs")
    index = lax.axis_index("pairs")
    first = index == 0
    last = index == count - 1
    pair = snapshots

    gram = allreduce_rows(gram_of(pair, pair)) / total
    sent, gram = lax.optimization_barrier((pair, gram))
    left = from_behind(sent[:, :width], "pairs", 1)
    right = lax.ppermute(sent[:, width:], "pairs", [(0, 1)])
    raw_a = jnp.where(first, pair, jnp.concatenate([left, right], axis=1))
    raw_b = jnp.where(last, pair, from_behind(sent, "pairs", -1))


    whiten = whitener(gram)
    head_w, tail_w = whiten[:width, :width], whiten[:, width:]
    moment_top = tmm(head_w, mm(gram[:width, :width], head_w))
    moment_bottom = tmm(tail_w, mm(gram, tail_w))
    top = jnp.concatenate([whiten[:, :width], moment_top], axis=0)
    bottom = jnp.concatenate([whiten[:, width:], moment_bottom], axis=0)
    outgoing = jnp.where(first, bottom, top)
    arrived_a = from_behind(outgoing, "pairs", 1)
    arrived_b = from_behind(bottom, "pairs", -1)
    side_a = jnp.where(first, top, arrived_a)
    side_b = jnp.where(last, top, arrived_b)
    rows = whiten.shape[0]
    x_a, m_a = side_a[:rows], side_a[rows:]
    x_b, m_b = side_b[:rows], side_b[rows:]

    off = allreduce_rows(tmm(x_a, mm(gram_of(raw_a, raw_b), x_b)), 1) / total
    gram2 = jnp.concatenate(
        [jnp.concatenate([m_a, off], axis=1), jnp.concatenate([off.T, m_b], axis=1)], axis=0
    )
    whiten2 = whitener(gram2)
    combined = jnp.concatenate([mm(x_a, whiten2[:width]), mm(x_b, whiten2[width:])], axis=0)
    return mm(jnp.concatenate([raw_a, raw_b], axis=1), combined)


def solution(mesh):
    return jax.shard_map(
        per_device,
        mesh=mesh,
        in_specs=(P("rows", "pairs"),),
        out_specs=P("rows", "pairs"),
        check_vma=False,
    )
```
